512 devices in a mesh: row: 16 (over y_hi, x), col: 32 (over z, y_lo, core).
Axes of the slice: x: 4, y: 8 (y_hi: 4, y_lo: 2; y = y_hi * 2 + y_lo), z: 8, core: 2. Of those that a mesh axis runs over, the one named last changes fastest.
Arguments:
- inputs: bfloat16 [4, 256, 256, 1280], P(None, 'row', 'col'), may hold values from -6 to 6
- cotangent: bfloat16 [4, 256, 256, 1280], P(None, 'row', 'col'), may hold values from -6 to 6
- w_in: bfloat16 [1474560], P(('row', 'col')), may hold values from -0.0546875 to 0.0546875
- w_out: bfloat16 [1474560], P(('row', 'col')), may hold values from -0.1875 to 0.1875
Outputs:
- input_grad: bfloat16 [4, 256, 256, 1280], P(None, 'row', 'col')
The draws below stay inside these ranges and needn't reach their ends.
All inputs are finite; a program needn't handle non-finite values.
Results may differ from the reference program's by a relative error of at most 0.0032.
Values may be sent and summed in bfloat16 or wider, within the bound.
A program may use at most 64 MiB of HBM per device.

```python
import jax
import jax.numpy as jnp
from jax import lax

C = 1280
MID = 128
BATCH = 4
HEIGHT = 256
WIDTH = 256


def block_levels(rng, extent, shards, least, largest):
    def one(position, blocks):
        heights = jax.random.uniform(jax.random.fold_in(jax.random.fold_in(rng, 6), position), (blocks,), jnp.float32, least / len(shards), largest / len(shards))
        return jnp.repeat(jnp.exp(heights), extent[position] // blocks).reshape((-1,) + (1,) * (len(extent) - position - 1))

    loudness = one(*shards[0])
    for cut in shards[1:]:
        loudness = loudness * one(*cut)
    return loudness


def scatter_about(stream_key, dims, scale, bound, pieces=(), held_as=jnp.bfloat16):
    drawn = scale * jax.random.normal(stream_key, dims, jnp.float32)
    if pieces:
        drawn = drawn * block_levels(stream_key, dims, pieces, -0.22, 0.18)
    return jnp.clip(drawn, -bound, bound).astype(held_as)


def setup_inputs(seed: int = 0) -> dict:
    arg_keys = jax.random.split(jax.random.key(seed), 5)
    inputs = scatter_about(arg_keys[0], (BATCH, HEIGHT, WIDTH, C), 1.0, 6.0, ((1, 16), (2, 32)))
    cotangent = scatter_about(arg_keys[1], (BATCH, HEIGHT, WIDTH, C), 1.0, 6.0, ((1, 16), (2, 32)))
    w_in = scatter_about(arg_keys[2], (9 * C * MID,), (9 * C) ** -0.5, 0.0546875, ((0, 512),))
    w_out = scatter_about(arg_keys[3], (9 * MID * C,), (9 * MID) ** -0.5, 0.1875, ((0, 512),))
    return dict(inputs=inputs, cotangent=cotangent, w_in=w_in, w_out=w_out)


def convolve(padded, kernel):
    return lax.conv_general_dilated(padded.astype(jnp.float32), kernel.astype(jnp.float32), (1, 1), "VALID", dimension_numbers=("NHWC", "HWIO", "NHWC"), precision=lax.Precision.HIGHEST)


def border(image):
    return jnp.pad(image[None], ((0, 0), (1, 1), (1, 1), (0, 0)))


def reference(inputs, cotangent, w_in, w_out):
    ker_in = w_in.reshape(3, 3, C, MID)
    ker_out = w_out.reshape(3, 3, MID, C)
    out_back = ker_out[::-1, ::-1].transpose(0, 1, 3, 2)
    in_back = ker_in[::-1, ::-1].transpose(0, 1, 3, 2)

    def single(pair):
        image, grad_image = pair
        pre = convolve(border(image), ker_in)[0]
        back_mid = convolve(border(grad_image), out_back)[0]
        sig = jax.nn.sigmoid(pre)
        grad_mid = (back_mid * (sig * (1.0 + pre * (1.0 - sig)))).astype(jnp.bfloat16)
        result = grad_image.astype(jnp.float32) + convolve(border(grad_mid), in_back)[0]
        return result.astype(jnp.bfloat16)

    return lax.map(single, (inputs, cotangent))
```

```python
import jax
import jax.numpy as jnp
from jax import lax
from jax.experimental import pallas as pl
from jax.experimental.pallas import tpu as pltpu
from jax.sharding import PartitionSpec as P

C = 1280
MID = 128
MESH = pl.DeviceIdType.MESH
CHUNK = 24
GROUP = 800

ORDER = [
    ("0", 0),
    ("0", 1), ("0", 3), ("o", 0),
    ("0", 2), ("o", 1), ("o", 3), ("i", 0),
    ("o", 2), ("i", 1), ("i", 3), ("2", 0),
    ("i", 2), ("2", 1), ("2", 3),
    ("2", 2),
]


def gather_kernel(w_ref, out_ref, raw, flat, blocks, zsend, zrecv, ysem, bsend, brecv, psend, precv, lsem):
    row, col = lax.axis_index("row"), lax.axis_index("col")
    h, x = row // 4, row % 4
    z, l, c = col // 4, (col // 2) % 2, col % 2
    sigma = 2 * l - 1

    def at(hh, xx, zz, ll, cc):
        return (hh * 4 + xx, zz * 4 + ll * 2 + cc)

    right = at(h, (x + 1) % 4, z, l, c)
    left = at(h, (x + 3) % 4, z, l, c)
    outer = at((h + sigma + 4) % 4, x, z, 1 - l, c)
    inner = at(h, x, z, 1 - l, c)
    partner = at(h, x, z, l, 1 - c)
    line = [(dz, dc) for dz in (0, 1, 7, 2, 6, 3, 5, 4) for dc in (0, 1) if (dz, dc) != (0, 0)]

    barrier = pltpu.get_barrier_semaphore()
    peers = [at(h, x, (z + dz) % 8, l, (c + dc) % 2) for dz, dc in line] + [right, left, outer, inner]
    for peer in peers:
        pl.semaphore_signal(barrier, inc=1, device_id=peer, device_id_type=MESH)
    pl.semaphore_wait(barrier, len(peers))

    own = pltpu.make_async_copy(w_ref.at[c], raw.at[l, z, c], lsem)
    own.start()
    sends = []
    for n, (dz, dc) in enumerate(line):
        to = (c + dc) % 2
        copy = pltpu.make_async_remote_copy(
            src_ref=w_ref.at[to], dst_ref=raw.at[l, z, c],
            send_sem=zsend.at[n], recv_sem=zrecv.at[z, c],
            device_id=at(h, x, (z + dz) % 8, l, to), device_id_type=MESH,
        )
        copy.start()
        sends.append(copy)
    own.wait()
    for dz, dc in line:
        zz, cc = (z + dz) % 8, (c + dc) % 2
        pltpu.make_async_remote_copy(
            src_ref=raw.at[l, zz, cc], dst_ref=raw.at[l, zz, cc],
            send_sem=zsend.at[0], recv_sem=zrecv.at[zz, cc],
            device_id=partner, device_id_type=MESH,
        ).wait_recv()

    swap = pltpu.make_async_remote_copy(
        src_ref=raw.at[l], dst_ref=raw.at[l], send_sem=ysem.at[0], recv_sem=ysem.at[1],
        device_id=inner, device_id_type=MESH,
    )
    swap.start()
    swap.wait()

    lanes = lax.broadcasted_iota(jnp.int32, (23, 128), 1)
    for i in range(16):
        even = raw[i % 2, i // 2, 0].astype(jnp.float32)
        odd = pltpu.roll(raw[i % 2, i // 2, 1].astype(jnp.float32), 64, 1)
        low = jnp.concatenate([even[22:23], odd[0:22]], axis=0)
        flat[45 * i:45 * i + 22] = even[0:22]
        flat[45 * i + 22:45 * i + 45] = jnp.where(lanes < 64, low, odd[0:23])
    mine = h * 4 + x

    @pl.when(c == 0)
    def _():
        blocks[0, mine, 0:720] = flat[0:720].astype(jnp.bfloat16)
        blocks[0, mine, 720:800] = jnp.zeros((80, 128), jnp.bfloat16)

    @pl.when(c == 1)
    def _():
        gap = jnp.zeros((8, 128), jnp.float32)
        for j in range(10):
            part = flat[pl.ds(j, 72, stride=10), :]
            moved = jnp.where(x % 2 == 1, jnp.concatenate([gap, part]), jnp.concatenate([part, gap]))
            blocks[1, mine, 80 * j:80 * j + 80] = moved.astype(jnp.bfloat16)

    forward = 1 - l
    waits = []
    for n, (dh, dx) in enumerate(ORDER):
        hh = {"0": h, "o": (h + sigma + 4) % 4, "i": (h - sigma + 4) % 4, "2": (h + 2) % 4}[dh]
        xx = (x + dx) % 4
        g = hh * 4 + xx
        block = blocks.at[c, g]

        def copy_to(device, slot):
            return pltpu.make_async_remote_copy(
                src_ref=block, dst_ref=block, send_sem=bsend.at[n, slot], recv_sem=brecv.at[g],
                device_id=device, device_id_type=MESH,
            )

        if n:
            copy_to(partner, 0).wait_recv()
        xfirst, yfirst = c == 0, c == 1
        same = xx % 2 == forward
        along_y = {"0": None, "o": None, "i": same, "2": jnp.logical_not(same)}[dh]
        y_to, y_slot = (outer, 0) if dh in ("0", "i") else (inner, 1)
        plan = []
        if dx == 0:
            plan.append((y_to, y_slot, along_y))
        else:
            plan.append((y_to, y_slot, xfirst if along_y is None else jnp.logical_and(xfirst, along_y)))
        along_x = None if dh == "0" else yfirst
        if dx == 0:
            plan += [(right, 2, along_x), (left, 3, along_x)]
        elif dx == 1:
            odd = hh % 2 == 1
            plan.append((left, 3, odd if along_x is None else jnp.logical_and(odd, along_x)))
        elif dx == 3:
            even = hh % 2 == 0
            plan.append((right, 2, even if along_x is None else jnp.logical_and(even, along_x)))
        for device, slot, when in plan:
            copy = copy_to(device, slot)
            if when is None:
                copy.start()
            else:
                pl.when(when)(copy.start)
            waits.append((copy, when))
        share = pltpu.make_async_remote_copy(
            src_ref=block, dst_ref=block, send_sem=psend.at[n], recv_sem=precv.at[g],
            device_id=partner, device_id_type=MESH,
        )
        share.start()
        waits.append((share, None))

    for g in range(16):
        pltpu.make_async_remote_copy(
            src_ref=blocks.at[1 - c, g], dst_ref=blocks.at[1 - c, g], send_sem=psend.at[0],
            recv_sem=precv.at[g], device_id=partner, device_id_type=MESH,
        ).wait_recv()
    result = pltpu.make_async_copy(blocks, out_ref, lsem)
    result.start()
    for copy in sends:
        copy.wait_send()
    for copy, when in waits:
        if when is None:
            copy.wait_send()
        else:
            pl.when(when)(copy.wait_send)
    result.wait()


def gathered(w):
    dma = pltpu.SemaphoreType.DMA
    return pl.pallas_call(
        gather_kernel,
        out_shape=jax.ShapeDtypeStruct((2, 16, GROUP, 128), jnp.bfloat16),
        in_specs=[pl.BlockSpec(memory_space=pltpu.VMEM)],
        out_specs=pl.BlockSpec(memory_space=pl.ANY),
        scratch_shapes=[
            pltpu.VMEM((2, 8, 2, CHUNK, 128), jnp.bfloat16),
            pltpu.VMEM((720, 128), jnp.float32),
            pltpu.VMEM((2, 16, GROUP, 128), jnp.bfloat16),
            dma((15,)), dma((8, 2)), dma((2,)), dma((16, 4)), dma((16,)), dma((16,)), dma((16,)), dma,
        ],
        compiler_params=pltpu.CompilerParams(
            collective_id=0, has_side_effects=True, vmem_limit_bytes=32 << 20
        ),
    )(w)


def padded_2(block, sides, width):
    for axis, dim in sides:
        count = lax.axis_size(axis)
        forward = [(i, i + 1) for i in range(count - 1)]
        backward = [(target, source) for source, target in forward]
        low = lax.ppermute(
            lax.slice_in_dim(block, block.shape[dim] - width, None, axis=dim), axis, forward
        )
        high = lax.ppermute(lax.slice_in_dim(block, 0, width, axis=dim), axis, backward)
        block = jnp.concatenate([low, block, high], axis=dim)
    return block


def convolve(padded, kernel):
    return lax.conv_general_dilated(
        padded,
        kernel,
        (1, 1),
        "VALID",
        dimension_numbers=("NHWC", "HWIO", "NHWC"),
        preferred_element_type=jnp.float32,
    )


def shards(inputs, cotangent, w_in, w_out):
    w = jnp.pad(jnp.stack([w_in, w_out]), ((0, 0), (0, CHUNK * 128 - 2880))).reshape(2, CHUNK, 128)
    full = gathered(w)
    ker_in = full[0, :, :720].reshape(3, 3, C, MID)
    pairs = full[1].reshape(8, 2, 10, 80, 128)
    rows = jnp.concatenate([pairs[:, 0, :, :72], pairs[:, 1, :, 8:]], axis=2)
    ker_out = rows.transpose(0, 2, 1, 3).reshape(3, 3, MID, C)
    pad_input = padded_2(inputs, (("row", 1), ("col", 2)), 1)
    pre = convolve(pad_input, ker_in)
    out_back = ker_out[::-1, ::-1].transpose(0, 1, 3, 2)
    pad_cotangent = padded_2(cotangent, (("row", 1), ("col", 2)), 1)
    back_mid = convolve(pad_cotangent, out_back)
    sigmoid_pre = jax.nn.sigmoid(pre)
    grad_mid = (back_mid * (sigmoid_pre * (1.0 + pre * (1.0 - sigmoid_pre)))).astype(jnp.bfloat16)
    pad_grad = padded_2(grad_mid, (("row", 1), ("col", 2)), 1)
    in_back = ker_in[::-1, ::-1].transpose(0, 1, 3, 2)
    result = cotangent.astype(jnp.float32) + convolve(pad_grad, in_back)
    return result.astype(jnp.bfloat16)


def solution(mesh):
    return jax.shard_map(
        shards,
        mesh=mesh,
        in_specs=(
            P(None, "row", "col", None),
            P(None, "row", "col", None),
            P(("row", "col")),
            P(("row", "col")),
        ),
        out_specs=P(None, "row", "col", None),
        check_vma=False,
    )
```

```python
import jax
import jax.numpy as jnp
from jax import lax
from jax.experimental import pallas as pl
from jax.experimental.pallas import tpu as pltpu
from jax.sharding import PartitionSpec as P

C = 1280
MESH = pl.DeviceIdType.MESH
CHUNK = 24
GROUP = 800

ORDER = [
    ("0", 0),
    ("0", 1), ("0", 3), ("o", 0),
    ("0", 2), ("o", 1), ("o", 3), ("i", 0),
    ("o", 2), ("i", 1), ("i", 3), ("2", 0),
    ("i", 2), ("2", 1), ("2", 3),
    ("2", 2),
]


def adapter_kernel(
    w_ref, in_ref, cot_ref, out_ref,
    raw, flat, blocks, maps, edge, cols, prod, beside, down, upk, grad, ghalo, gsend, grecv, gcol, shifted, lhs, result,
    zsend, zrecv, ysem, bsend, brecv, psend, precv, xsend, xrecv, hsend, hrecv, lsem, osem,
):
    row, col = lax.axis_index("row"), lax.axis_index("col")
    h, x = row // 4, row % 4
    z, l, c = col // 4, (col // 2) % 2, col % 2
    sigma = 2 * l - 1

    def at(hh, xx, zz, ll, cc):
        return (hh * 4 + xx, zz * 4 + ll * 2 + cc)

    right = at(h, (x + 1) % 4, z, l, c)
    left = at(h, (x + 3) % 4, z, l, c)
    outer = at((h + sigma + 4) % 4, x, z, 1 - l, c)
    inner = at(h, x, z, 1 - l, c)
    partner = at(h, x, z, l, 1 - c)
    line = [(dz, dc) for dz in (0, 1, 7, 2, 6, 3, 5, 4) for dc in (0, 1) if (dz, dc) != (0, 0)]

    has_up, has_down, has_left, has_right = row > 0, row < 15, col > 0, col < 31
    both = jnp.logical_and
    around = [
        (has_up, (row - 1, col)), (has_down, (row + 1, col)),
        (has_left, (row, col - 1)), (has_right, (row, col + 1)),
        (both(has_up, has_left), (row - 1, col - 1)), (both(has_up, has_right), (row - 1, col + 1)),
        (both(has_down, has_left), (row + 1, col - 1)), (both(has_down, has_right), (row + 1, col + 1)),
    ]
    opposite = (1, 0, 3, 2, 7, 6, 5, 4)

    barrier = pltpu.get_barrier_semaphore()
    peers = [at(h, x, (z + dz) % 8, l, (c + dc) % 2) for dz, dc in line] + [right, left, outer, inner]
    for peer in peers:
        pl.semaphore_signal(barrier, inc=1, device_id=peer, device_id_type=MESH)
    for exists, device in around:
        @pl.when(exists)
        def _():
            pl.semaphore_signal(barrier, inc=1, device_id=device, device_id_type=MESH)
    pl.semaphore_wait(barrier, len(peers) + sum(exists.astype(jnp.int32) for exists, _ in around))

    own = pltpu.make_async_copy(w_ref.at[c], raw.at[l, z, c], lsem.at[0])
    own.start()
    sends = []
    for n, (dz, dc) in enumerate(line):
        to = (c + dc) % 2
        copy = pltpu.make_async_remote_copy(
            src_ref=w_ref.at[to], dst_ref=raw.at[l, z, c],
            send_sem=zsend.at[n], recv_sem=zrecv.at[z, c],
            device_id=at(h, x, (z + dz) % 8, l, to), device_id_type=MESH,
        )
        copy.start()
        sends.append(copy)
    local = [
        pltpu.make_async_copy(ref, maps.at[n, :, 1:17], lsem.at[1 + n]) for n, ref in enumerate((in_ref, cot_ref))
    ]
    for copy in local:
        copy.start()

    def map_row(n, d, ref):
        return pltpu.make_async_remote_copy(
            src_ref=ref.at[:, 15 * d], dst_ref=maps.at[n, :, 17 - 17 * d],
            send_sem=xsend.at[n, d], recv_sem=xrecv.at[n, opposite[d]],
            device_id=around[d][1], device_id_type=MESH,
        )

    def map_row_in(n, d, ref):
        return pltpu.make_async_remote_copy(
            src_ref=ref.at[:, 0], dst_ref=maps.at[n, :, 17 * d],
            send_sem=xsend.at[n, d], recv_sem=xrecv.at[n, d],
            device_id=around[d][1], device_id_type=MESH,
        )

    for n, ref in enumerate((in_ref, cot_ref)):
        for d in range(2):
            pl.when(around[d][0])(map_row(n, d, ref).start)

            @pl.when(jnp.logical_not(around[d][0]))
            def _():
                maps[n, :, 17 * d] = jnp.zeros((4, 8, C), jnp.bfloat16)
    own.wait()
    for dz, dc in line:
        zz, cc = (z + dz) % 8, (c + dc) % 2
        pltpu.make_async_remote_copy(
            src_ref=raw.at[l, zz, cc], dst_ref=raw.at[l, zz, cc],
            send_sem=zsend.at[0], recv_sem=zrecv.at[zz, cc],
            device_id=partner, device_id_type=MESH,
        ).wait_recv()

    swap = pltpu.make_async_remote_copy(
        src_ref=raw.at[l], dst_ref=raw.at[l], send_sem=ysem.at[0], recv_sem=ysem.at[1],
        device_id=inner, device_id_type=MESH,
    )
    swap.start()
    swap.wait()

    lanes = lax.broadcasted_iota(jnp.int32, (23, 128), 1)
    for i in range(16):
        even = raw[i % 2, i // 2, 0].astype(jnp.float32)
        odd = pltpu.roll(raw[i % 2, i // 2, 1].astype(jnp.float32), 64, 1)
        low = jnp.concatenate([even[22:23], odd[0:22]], axis=0)
        flat[45 * i:45 * i + 22] = even[0:22]
        flat[45 * i + 22:45 * i + 45] = jnp.where(lanes < 64, low, odd[0:23])
    mine = h * 4 + x

    @pl.when(c == 0)
    def _():
        blocks[0, mine, 0:720] = flat[0:720].astype(jnp.bfloat16)
        blocks[0, mine, 720:800] = jnp.zeros((80, 128), jnp.bfloat16)

    @pl.when(c == 1)
    def _():
        gap = jnp.zeros((8, 128), jnp.float32)
        for j in range(10):
            part = flat[pl.ds(j, 72, stride=10), :]
            moved = jnp.where(x % 2 == 1, jnp.concatenate([gap, part]), jnp.concatenate([part, gap]))
            blocks[1, mine, 80 * j:80 * j + 80] = moved.astype(jnp.bfloat16)

    def column(n, side):
        return pltpu.make_async_remote_copy(
            src_ref=edge.at[n, side], dst_ref=cols.at[n, 1 - side],
            send_sem=xsend.at[n, 2 + side], recv_sem=xrecv.at[n, 3 - side],
            device_id=around[2 + side][1], device_id_type=MESH,
        )

    def column_in(n, side):
        return pltpu.make_async_remote_copy(
            src_ref=edge.at[n, side], dst_ref=cols.at[n, side],
            send_sem=xsend.at[n, 2 + side], recv_sem=xrecv.at[n, 2 + side],
            device_id=around[2 + side][1], device_id_type=MESH,
        )

    def border_columns():
        wanted = lax.broadcasted_iota(jnp.int32, (160, 576), 0)
        wanted = jnp.where(wanted < 80, wanted * 8, (wanted - 80) * 8 + 7)
        pick = jnp.where(lax.broadcasted_iota(jnp.int32, (160, 576), 1) == wanted, 1.0, 0.0).astype(jnp.bfloat16)
        for n, ref in enumerate((in_ref, cot_ref)):
            local[n].wait()
            for d in range(2):
                pl.when(around[d][0])(map_row_in(n, d, ref).wait_recv)
            picked = jnp.dot(pick, maps[n].reshape(576, C), preferred_element_type=jnp.float32)
            edge[n] = picked.astype(jnp.bfloat16).reshape(2, 80, C)
        for n in range(2):
            for side in range(2):
                pl.when(around[2 + side][0])(column(n, side).start)

                @pl.when(jnp.logical_not(around[2 + side][0]))
                def _():
                    cols[n, side] = jnp.zeros((80, C), jnp.bfloat16)

    forward = 1 - l
    waits = []
    for n, (dh, dx) in enumerate(ORDER):
        hh = {"0": h, "o": (h + sigma + 4) % 4, "i": (h - sigma + 4) % 4, "2": (h + 2) % 4}[dh]
        xx = (x + dx) % 4
        g = hh * 4 + xx
        block = blocks.at[c, g]

        def copy_to(device, slot):
            return pltpu.make_async_remote_copy(
                src_ref=block, dst_ref=block, send_sem=bsend.at[n, slot], recv_sem=brecv.at[g],
                device_id=device, device_id_type=MESH,
            )

        if n:
            copy_to(partner, 0).wait_recv()
        xfirst, yfirst = c == 0, c == 1
        same = xx % 2 == forward
        along_y = {"0": None, "o": None, "i": same, "2": jnp.logical_not(same)}[dh]
        y_to, y_slot = (outer, 0) if dh in ("0", "i") else (inner, 1)
        plan = []
        if dx == 0:
            plan.append((y_to, y_slot, along_y))
        else:
            plan.append((y_to, y_slot, xfirst if along_y is None else jnp.logical_and(xfirst, along_y)))
        along_x = None if dh == "0" else yfirst
        if dx == 0:
            plan += [(right, 2, along_x), (left, 3, along_x)]
        elif dx == 1:
            odd = hh % 2 == 1
            plan.append((left, 3, odd if along_x is None else jnp.logical_and(odd, along_x)))
        elif dx == 3:
            even = hh % 2 == 0
            plan.append((right, 2, even if along_x is None else jnp.logical_and(even, along_x)))
        for device, slot, when in plan:
            copy = copy_to(device, slot)
            if when is None:
                copy.start()
            else:
                pl.when(when)(copy.start)
            waits.append((copy, when))
        share = pltpu.make_async_remote_copy(
            src_ref=block, dst_ref=block, send_sem=psend.at[n], recv_sem=precv.at[g],
            device_id=partner, device_id_type=MESH,
        )
        share.start()
        waits.append((share, None))
        if n == 0:
            border_columns()

    for g in range(16):
        pltpu.make_async_remote_copy(
            src_ref=blocks.at[1 - c, g], dst_ref=blocks.at[1 - c, g], send_sem=psend.at[0],
            recv_sem=precv.at[g], device_id=partner, device_id_type=MESH,
        ).wait_recv()
    for g in range(16):
        down[720 * g:720 * g + 720] = blocks[0, g, 0:720]
    down[11520:12800] = jnp.zeros((1280, 128), jnp.bfloat16)
    for tap in range(9):
        for j in range(10):
            pieces, first = [], 128 * tap
            while first < 128 * tap + 128:
                g, at_row = divmod(first, 72)
                last = min(72 * g + 72, 128 * tap + 128)
                start = 80 * j + 8 * (g % 2) + at_row
                pieces.append(blocks[1, g, start:start + last - first].astype(jnp.float32))
                first = last
            upk[128 * (8 - tap):128 * (8 - tap) + 128, 128 * j:128 * j + 128] = (
                jnp.concatenate(pieces, axis=0).astype(jnp.bfloat16)
            )
    upk[1152:1280] = jnp.zeros((128, C), jnp.bfloat16)
    for n in range(2):
        for side in range(2):
            pl.when(around[2 + side][0])(column_in(n, side).wait_recv)

    pixels = [
        jnp.concatenate([maps[n].reshape(576, C), cols[n].reshape(160, C)], axis=0) for n in range(2)
    ]

    def two_taps(step, carry):
        first = pl.multiple_of(step * 2560, 2560)
        two = jnp.concatenate([down[pl.ds(first, C)], down[pl.ds(first + C, C)]], axis=1)
        out = pl.ds(pl.multiple_of(step * 256, 256), 256)
        prod[0, :, out] = jnp.dot(pixels[0], two, preferred_element_type=jnp.float32)
        rows = upk[pl.ds(pl.multiple_of(step * 256, 256), 256)]
        prod[1, :, out] = lax.dot_general(
            pixels[1], rows, (((1,), (1,)), ((), ())), preferred_element_type=jnp.float32
        )
        return carry

    lax.fori_loop(0, 5, two_taps, 0)

    lane_row = lax.broadcasted_iota(jnp.int32, (8, 128), 0)
    for n in range(2):
        for side in range(2):
            three = [
                prod[n, 576 + 80 * side:656 + 80 * side, 128 * (3 * a + 2 * side):128 * (3 * a + 2 * side) + 128]
                for a in range(3)
            ]
            for b in range(4):
                terms = [three[a][18 * b + a:18 * b + a + 16] for a in range(3)]
                beside[n, side, 16 * b:16 * b + 16] = terms[0] + terms[1] + terms[2]

    def pixel_row(i, carry):
        b, r = i // 16, i % 16
        sums = []
        for n in range(2):
            three = []
            for e in range(3):
                terms = [
                    prod[n, pl.ds(pl.multiple_of((b * 18 + r + a) * 8, 8), 8), 128 * (3 * a + e):128 * (3 * a + e) + 128]
                    for a in range(3)
                ]
                three.append(terms[0] + terms[1] + terms[2])
            sides = [beside[n, side, pl.ds(i, 1)] for side in range(2)]
            sums.append(
                jnp.where(lane_row == 0, sides[0], pltpu.roll(three[0], 1, 0))
                + three[1]
                + jnp.where(lane_row == 7, sides[1], pltpu.roll(three[2], 7, 0))
            )
        pre, back = sums
        s = jax.nn.sigmoid(pre)
        value = (back * (s * (1.0 + pre * (1.0 - s)))).astype(jnp.bfloat16)
        grad[b, 1 + r] = value
        value = value.astype(jnp.float32)
        gcol[0, pl.ds(i, 1)] = value[0:1]
        gcol[1, pl.ds(i, 1)] = value[7:8]
        return carry

    lax.fori_loop(0, 64, pixel_row, 0)

    for side in range(2):
        gsend[side] = gcol[side, 0:64].astype(jnp.bfloat16)
        for k in range(2):
            corner = [gcol[side, 16 * b + 15 * k:16 * b + 15 * k + 1] for b in range(4)]
            corner = jnp.concatenate(corner + [jnp.zeros((12, 128), jnp.float32)], axis=0)
            gsend[2 + 2 * k + side, 0:16] = corner.astype(jnp.bfloat16)

    def grad_border(d, to):
        if d < 2:
            src, dst = grad.at[:, 1 + 15 * d], grad.at[:, 17 - 17 * d]
            if not to:
                dst = grad.at[:, 17 * d]
        elif d < 4:
            src = gsend.at[d - 2, 0:64]
            dst = grecv.at[(3 - d) if to else (d - 2), 0:64]
        else:
            src = gsend.at[d - 2, 0:16]
            dst = grecv.at[(opposite[d] if to else d) - 2, 0:16]
        return pltpu.make_async_remote_copy(
            src_ref=src, dst_ref=dst, send_sem=hsend.at[d], recv_sem=hrecv.at[opposite[d] if to else d],
            device_id=around[d][1], device_id_type=MESH,
        )

    for d in range(8):
        pl.when(around[d][0])(grad_border(d, True).start)
    for d in range(8):
        @pl.when(jnp.logical_not(around[d][0]))
        def _():
            if d < 2:
                grad[:, 17 * d] = jnp.zeros((4, 8, 128), jnp.bfloat16)
            elif d < 4:
                grecv[d - 2] = jnp.zeros((64, 128), jnp.bfloat16)
            else:
                grecv[d - 2, 0:16] = jnp.zeros((16, 128), jnp.bfloat16)
    for d in range(8):
        pl.when(around[d][0])(grad_border(d, False).wait_recv)

    for side in range(2):
        middle = grecv[side].astype(jnp.float32)
        top = grecv[2 + side, 0:16].astype(jnp.float32)
        bottom = grecv[4 + side, 0:16].astype(jnp.float32)
        for b in range(4):
            ghalo[side, 18 * b:18 * b + 18] = jnp.concatenate(
                [top[b:b + 1], middle[16 * b:16 * b + 16], bottom[b:b + 1]], axis=0
            )

    def shift_row(i, carry):
        b, r = i // 18, i % 18
        value = grad[b, r].astype(jnp.float32)
        before, after = ghalo[0, pl.ds(i, 1)], ghalo[1, pl.ds(i, 1)]
        shifted[0, b, r] = jnp.where(lane_row == 7, after, pltpu.roll(value, 7, 0)).astype(jnp.bfloat16)
        shifted[1, b, r] = grad[b, r]
        shifted[2, b, r] = jnp.where(lane_row == 0, before, pltpu.roll(value, 1, 0)).astype(jnp.bfloat16)
        return carry

    lax.fori_loop(0, 72, shift_row, 0)
    for tap in range(9):
        a, e = divmod(tap, 3)
        lhs[:, 128 * tap:128 * tap + 128] = shifted[e, :, 2 - a:18 - a].reshape(512, 128)

    def channels(step, carry):
        first = pl.multiple_of(step * 256, 256)
        weights = jnp.concatenate(
            [down[pl.ds(pl.multiple_of(C * tap + first, 256), 256)] for tap in range(9)], axis=1
        )
        out = lax.dot_general(lhs[...], weights, (((1,), (1,)), ((), ())), preferred_element_type=jnp.float32)
        kept = maps[1, :, 1:17, :, pl.ds(first, 256)].reshape(512, 256).astype(jnp.float32)
        result[:, pl.ds(first, 256)] = (out + kept).astype(jnp.bfloat16)
        return carry

    lax.fori_loop(0, 5, channels, 0)
    final = pltpu.make_async_copy(result, out_ref, osem)
    final.start()
    for copy in sends:
        copy.wait_send()
    for copy, when in waits:
        if when is None:
            copy.wait_send()
        else:
            pl.when(when)(copy.wait_send)
    for n, ref in enumerate((in_ref, cot_ref)):
        for d in range(2):
            pl.when(around[d][0])(map_row(n, d, ref).wait_send)
            pl.when(around[2 + d][0])(column(n, d).wait_send)
    for d in range(8):
        pl.when(around[d][0])(grad_border(d, True).wait_send)
    final.wait()


def solution(mesh):
    dma = pltpu.SemaphoreType.DMA
    bf16, f32 = jnp.bfloat16, jnp.float32

    def shards(inputs, cotangent, w_in, w_out):
        w = jnp.pad(jnp.stack([w_in, w_out]), ((0, 0), (0, CHUNK * 128 - 2880))).reshape(2, CHUNK, 128)
        result = pl.pallas_call(
            adapter_kernel,
            out_shape=jax.ShapeDtypeStruct((512, C), bf16),
            in_specs=[
                pl.BlockSpec(memory_space=pltpu.VMEM),
                pl.BlockSpec(memory_space=pl.ANY),
                pl.BlockSpec(memory_space=pl.ANY),
            ],
            out_specs=pl.BlockSpec(memory_space=pl.ANY),
            scratch_shapes=[
                pltpu.VMEM((2, 8, 2, CHUNK, 128), bf16),
                pltpu.VMEM((720, 128), f32),
                pltpu.VMEM((2, 16, GROUP, 128), bf16),
                pltpu.VMEM((2, 4, 18, 8, C), bf16),
                pltpu.VMEM((2, 2, 80, C), bf16),
                pltpu.VMEM((2, 2, 80, C), bf16),
                pltpu.VMEM((2, 736, 1280), f32),
                pltpu.VMEM((2, 2, 64, 128), f32),
                pltpu.VMEM((12800, 128), bf16),
                pltpu.VMEM((1280, C), bf16),
                pltpu.VMEM((4, 18, 8, 128), bf16),
                pltpu.VMEM((2, 72, 128), f32),
                pltpu.VMEM((6, 64, 128), bf16),
                pltpu.VMEM((6, 64, 128), bf16),
                pltpu.VMEM((2, 64, 128), f32),
                pltpu.VMEM((3, 4, 18, 8, 128), bf16),
                pltpu.VMEM((512, 1152), bf16),
                pltpu.VMEM((512, C), bf16),
                dma((15,)), dma((8, 2)), dma((2,)), dma((16, 4)), dma((16,)), dma((16,)), dma((16,)),
                dma((2, 4)), dma((2, 4)), dma((8,)), dma((8,)), dma((3,)), dma,
            ],
            compiler_params=pltpu.CompilerParams(
                collective_id=0, has_side_effects=True, vmem_limit_bytes=56 << 20
            ),
        )(w, inputs, cotangent)
        return result.reshape(4, 16, 8, C)

    spec = P(None, "row", "col", None)
    flat = P(("row", "col"))
    return jax.shard_map(
        shards, mesh=mesh, in_specs=(spec, spec, flat, flat), out_specs=spec, check_vma=False
    )
```

```python
import jax
import jax.numpy as jnp
from jax import lax
from jax.experimental import pallas as pl
from jax.experimental.pallas import tpu as pltpu
from jax.sharding import PartitionSpec as P

C = 1280
MESH = pl.DeviceIdType.MESH
CHUNK = 24
FRAME = 192
LAG = 6

ORDER = [
    (0, 0),
    (1, 0), (3, 0), (0, 1), (0, -1), (2, 0), (0, 2), (0, -2),
    (1, 1), (1, -1), (3, 1), (3, -1), (1, 2), (1, -2), (3, 2), (3, -2),
    (2, 1), (2, -1), (2, 2), (2, -2), (0, 3), (0, -3), (0, 4),
    (1, 3), (1, -3), (3, 3), (3, -3), (2, 3), (2, -3), (1, 4), (3, 4), (2, 4),
]


def adapter_kernel(
    win_ref, wout_ref, in_ref, cot_ref, out_ref,
    raw, flat, units, maps, edge, cols, prod, beside, down, uflat, utap, upk, grad, ghalo, gsend, grecv, gcol, shifted, lhs, result,
    rsend, rrecv, usend, urecv, zrecv, psend, precv, xsend, xrecv, hsend, hrecv, lsem, osem,
):
    row, col = lax.axis_index("row"), lax.axis_index("col")
    h, x = row // 4, row % 4
    z, l, c = col // 4, (col // 2) % 2, col % 2
    y, zp = 2 * h + l, z % 2
    quarter, to_quarter = 2 * zp + l, z // 2
    both, no = jnp.logical_and, jnp.logical_not

    def at(xx, yy, zz, cc):
        return ((yy // 2) * 4 + xx, zz * 4 + (yy % 2) * 2 + cc)

    def along_x(d):
        return at((x + d) % 4, y, z, c)

    def along_y(d):
        return at(x, (y + d + 8) % 8, z, c)

    partner = at(x, y, z, 1 - c)
    carriers = [
        (kk, at(x, 2 * h + to_quarter % 2, to_quarter // 2 + 2 * k, kk),
         both(both(to_quarter // 2 + 2 * k == z, to_quarter % 2 == l), c == kk))
        for k in range(4) for kk in range(2)
    ]
    carried = [
        (i, cc, at(x, 2 * h + i % 2, 2 * quarter + i // 2, cc),
         both(both(2 * quarter + i // 2 == z, i % 2 == l), c == cc))
        for i in range(4) for cc in range(2)
    ]

    has_up, has_down, has_left, has_right = row > 0, row < 15, col > 0, col < 31
    around = [
        (has_up, (row - 1, col)), (has_down, (row + 1, col)),
        (has_left, (row, col - 1)), (has_right, (row, col + 1)),
        (both(has_up, has_left), (row - 1, col - 1)), (both(has_up, has_right), (row - 1, col + 1)),
        (both(has_down, has_left), (row + 1, col - 1)), (both(has_down, has_right), (row + 1, col + 1)),
    ]
    opposite = (1, 0, 3, 2, 7, 6, 5, 4)

    barrier = pltpu.get_barrier_semaphore()
    peers = [along_x(d) for d in (1, 2, 3)] + [along_y(d) for d in (1, -1, 2, -2)]
    peers += [at(x, y, (z + d) % 8, c) for d in (1, 7)] + [partner]
    for peer in peers:
        pl.semaphore_signal(barrier, inc=1, device_id=peer, device_id_type=MESH)
    for _, _, device, itself in carried:
        @pl.when(no(itself))
        def _():
            pl.semaphore_signal(barrier, inc=1, device_id=device, device_id_type=MESH)
    for exists, device in around:
        @pl.when(exists)
        def _():
            pl.semaphore_signal(barrier, inc=1, device_id=device, device_id_type=MESH)
    arrivals = sum(exists.astype(jnp.int32) for exists, _ in around)
    arrivals += sum(no(itself).astype(jnp.int32) for _, _, itself in carriers)
    pl.semaphore_wait(barrier, len(peers) + arrivals)

    place = 2 * zp + l
    chunks = []
    for n, (kk, device, itself) in enumerate(carriers):
        source = (win_ref, wout_ref)[kk]
        copy = pltpu.make_async_remote_copy(
            src_ref=source, dst_ref=raw.at[place, c], send_sem=rsend.at[n], recv_sem=rrecv.at[place, c],
            device_id=device, device_id_type=MESH,
        )
        pl.when(no(itself))(copy.start)
        chunks.append((copy, no(itself)))
        pl.when(itself)(pltpu.make_async_copy(source, raw.at[place, c], lsem.at[0]).start)
    local = [
        pltpu.make_async_copy(ref, maps.at[n, :, 1:17], lsem.at[1 + n]) for n, ref in enumerate((in_ref, cot_ref))
    ]
    for copy in local:
        copy.start()

    def map_row(n, d, ref):
        return pltpu.make_async_remote_copy(
            src_ref=ref.at[:, 15 * d], dst_ref=maps.at[n, :, 17 - 17 * d],
            send_sem=xsend.at[n, d], recv_sem=xrecv.at[n, opposite[d]],
            device_id=around[d][1], device_id_type=MESH,
        )

    def map_row_in(n, d, ref):
        return pltpu.make_async_remote_copy(
            src_ref=ref.at[:, 0], dst_ref=maps.at[n, :, 17 * d],
            send_sem=xsend.at[n, d], recv_sem=xrecv.at[n, d],
            device_id=around[d][1], device_id_type=MESH,
        )

    for n, ref in enumerate((in_ref, cot_ref)):
        for d in range(2):
            pl.when(around[d][0])(map_row(n, d, ref).start)

            @pl.when(jnp.logical_not(around[d][0]))
            def _():
                maps[n, :, 17 * d] = jnp.zeros((4, 8, C), jnp.bfloat16)
    for i, cc, _, itself in carried:
        pl.when(no(itself))(pltpu.make_async_remote_copy(
            src_ref=raw.at[i, cc], dst_ref=raw.at[i, cc], send_sem=rsend.at[0], recv_sem=rrecv.at[i, cc],
            device_id=partner, device_id_type=MESH,
        ).wait_recv)
        pl.when(itself)(pltpu.make_async_copy(win_ref, raw.at[i, cc], lsem.at[0]).wait)

    lanes = lax.broadcasted_iota(jnp.int32, (23, 128), 1)
    pieces = []
    for i in range(4):
        even = raw[i, 0].astype(jnp.float32)
        odd = pltpu.roll(raw[i, 1].astype(jnp.float32), 64, 1)
        low = jnp.concatenate([even[22:23], odd[0:22]], axis=0)
        pieces.append((even[0:22], jnp.where(lanes < 64, low, odd[0:23])))
    flat[...] = jnp.zeros((FRAME, 128), jnp.float32)
    for k in range(4):
        @pl.when(quarter == k)
        def _():
            for i in range(4):
                first = 4 * k + 45 * i
                flat[first:first + 22] = pieces[i][0]
                flat[first + 22:first + 45] = pieces[i][1]
    units[c, x, y, zp] = flat[...].astype(jnp.bfloat16)

    def column(n, side):
        return pltpu.make_async_remote_copy(
            src_ref=edge.at[n, side], dst_ref=cols.at[n, 1 - side],
            send_sem=xsend.at[n, 2 + side], recv_sem=xrecv.at[n, 3 - side],
            device_id=around[2 + side][1], device_id_type=MESH,
        )

    def column_in(n, side):
        return pltpu.make_async_remote_copy(
            src_ref=edge.at[n, side], dst_ref=cols.at[n, side],
            send_sem=xsend.at[n, 2 + side], recv_sem=xrecv.at[n, 2 + side],
            device_id=around[2 + side][1], device_id_type=MESH,
        )

    def border_columns():
        wanted = lax.broadcasted_iota(jnp.int32, (160, 576), 0)
        wanted = jnp.where(wanted < 80, wanted * 8, (wanted - 80) * 8 + 7)
        pick = jnp.where(lax.broadcasted_iota(jnp.int32, (160, 576), 1) == wanted, 1.0, 0.0).astype(jnp.bfloat16)
        for n, ref in enumerate((in_ref, cot_ref)):
            local[n].wait()
            for d in range(2):
                pl.when(around[d][0])(map_row_in(n, d, ref).wait_recv)
            picked = jnp.dot(pick, maps[n].reshape(576, C), preferred_element_type=jnp.float32)
            edge[n] = picked.astype(jnp.bfloat16).reshape(2, 80, C)
        for n in range(2):
            for side in range(2):
                pl.when(around[2 + side][0])(column(n, side).start)

                @pl.when(jnp.logical_not(around[2 + side][0]))
                def _():
                    cols[n, side] = jnp.zeros((80, C), jnp.bfloat16)

    waits = []

    def send(unit, device, sends, receives, when):
        copy = pltpu.make_async_remote_copy(
            src_ref=unit, dst_ref=unit, send_sem=sends, recv_sem=receives,
            device_id=device, device_id_type=MESH,
        )
        if when is None:
            copy.start()
        else:
            pl.when(when)(copy.start)
        waits.append((copy, when))

    def arrived(unit, receives):
        pltpu.make_async_remote_copy(
            src_ref=unit, dst_ref=unit, send_sem=psend.at[0], recv_sem=receives,
            device_id=partner, device_id_type=MESH,
        ).wait_recv()

    def share(n, xx, yy, parity):
        send(units.at[c, xx, yy, parity], partner, psend.at[n], precv.at[xx, yy, parity], None)

    def from_z(n):
        dx, dy = ORDER[n]
        xx, yy = (x + dx) % 4, (y + dy + 8) % 8
        arrived(units.at[c, xx, yy, 1 - zp], zrecv.at[xx, yy])
        share(32 + n, xx, yy, 1 - zp)

    first, second = c == 0, c == 1
    for n, (dx, dy) in enumerate(ORDER):
        xx, yy = (x + dx) % 4, (y + dy + 8) % 8
        parity = (xx + yy) % 2
        unit = units.at[c, xx, yy, zp]
        if n:
            arrived(unit, urecv.at[xx, yy])
        steps = {0: (1, -1, 2, -2), -2: (1, 2), 2: (-1, -2)}.get(dy, ())
        for k, step in enumerate(steps):
            when = None if dx == 0 else first
            if dy and abs(step) == 2:
                chosen = parity == (0 if step > 0 else 1)
                when = chosen if when is None else both(when, chosen)
            send(unit, along_y(step), usend.at[n, k], urecv.at[xx, yy], when)
        if dx == 0:
            for k, step in enumerate((1, 3, 2)):
                send(unit, along_x(step), usend.at[n, 4 + k], urecv.at[xx, yy], None if dy == 0 else second)
        send(unit, at(x, y, (z + 1 + 6 * parity) % 8, c), usend.at[n, 7], zrecv.at[xx, yy], None)
        share(n, xx, yy, zp)
        if n == 0:
            border_columns()
        if n >= LAG:
            from_z(n - LAG)
    for n in range(32 - LAG, 32):
        from_z(n)
    for xx in range(4):
        for yy in range(8):
            for parity in range(2):
                arrived(units.at[1 - c, xx, yy, parity], precv.at[xx, yy, parity])

    frame_row = lax.broadcasted_iota(jnp.int32, (16, 128), 0)
    for k, whole in enumerate((down, uflat)):
        for g in range(16):
            frames = [units.at[k, g % 4, 2 * (g // 4) + q % 2, q // 2] for q in range(4)]
            for q in range(4):
                start = 720 * g + 176 * q
                last = FRAME if q == 3 else 176
                begin = 16 if q else 0
                whole[start + begin:start + last] = frames[q][begin:last]
                if q:
                    seam = jnp.where(
                        frame_row < 4 * q, frames[q - 1][176:192].astype(jnp.float32),
                        frames[q][0:16].astype(jnp.float32),
                    )
                    whole[start:start + 16] = seam.astype(jnp.bfloat16)
    down[11520:12800] = jnp.zeros((1280, 128), jnp.bfloat16)

    def up_tap(tap, carry):
        utap[...] = uflat[pl.ds(pl.multiple_of(tap * 1280, 1280), 1280)].astype(jnp.float32)
        for j in range(10):
            rows = utap[pl.ds(j, 128, stride=10), :].astype(jnp.bfloat16)
            upk[pl.ds(pl.multiple_of((8 - tap) * 128, 128), 128), 128 * j:128 * j + 128] = rows
        return carry

    lax.fori_loop(0, 9, up_tap, 0)
    upk[1152:1280] = jnp.zeros((128, C), jnp.bfloat16)
    for n in range(2):
        for side in range(2):
            pl.when(around[2 + side][0])(column_in(n, side).wait_recv)

    pixels = [
        jnp.concatenate([maps[n].reshape(576, C), cols[n].reshape(160, C)], axis=0) for n in range(2)
    ]

    def two_taps(step, carry):
        first = pl.multiple_of(step * 2560, 2560)
        two = jnp.concatenate([down[pl.ds(first, C)], down[pl.ds(first + C, C)]], axis=1)
        out = pl.ds(pl.multiple_of(step * 256, 256), 256)
        prod[0, :, out] = jnp.dot(pixels[0], two, preferred_element_type=jnp.float32)
        rows = upk[pl.ds(pl.multiple_of(step * 256, 256), 256)]
        prod[1, :, out] = lax.dot_general(
            pixels[1], rows, (((1,), (1,)), ((), ())), preferred_element_type=jnp.float32
        )
        return carry

    lax.fori_loop(0, 5, two_taps, 0)

    lane_row = lax.broadcasted_iota(jnp.int32, (8, 128), 0)
    for n in range(2):
        for side in range(2):
            three = [
                prod[n, 576 + 80 * side:656 + 80 * side, 128 * (3 * a + 2 * side):128 * (3 * a + 2 * side) + 128]
                for a in range(3)
            ]
            for b in range(4):
                terms = [three[a][18 * b + a:18 * b + a + 16] for a in range(3)]
                beside[n, side, 16 * b:16 * b + 16] = terms[0] + terms[1] + terms[2]

    def pixel_row(i, carry):
        b, r = i // 16, i % 16
        sums = []
        for n in range(2):
            three = []
            for e in range(3):
                terms = [
                    prod[n, pl.ds(pl.multiple_of((b * 18 + r + a) * 8, 8), 8), 128 * (3 * a + e):128 * (3 * a + e) + 128]
                    for a in range(3)
                ]
                three.append(terms[0] + terms[1] + terms[2])
            sides = [beside[n, side, pl.ds(i, 1)] for side in range(2)]
            sums.append(
                jnp.where(lane_row == 0, sides[0], pltpu.roll(three[0], 1, 0))
                + three[1]
                + jnp.where(lane_row == 7, sides[1], pltpu.roll(three[2], 7, 0))
            )
        pre, back = sums
        s = jax.nn.sigmoid(pre)
        value = (back * (s * (1.0 + pre * (1.0 - s)))).astype(jnp.bfloat16)
        grad[b, 1 + r] = value
        value = value.astype(jnp.float32)
        gcol[0, pl.ds(i, 1)] = value[0:1]
        gcol[1, pl.ds(i, 1)] = value[7:8]
        return carry

    lax.fori_loop(0, 64, pixel_row, 0)

    for side in range(2):
        gsend[side] = gcol[side, 0:64].astype(jnp.bfloat16)
        for k in range(2):
            corner = [gcol[side, 16 * b + 15 * k:16 * b + 15 * k + 1] for b in range(4)]
            corner = jnp.concatenate(corner + [jnp.zeros((12, 128), jnp.float32)], axis=0)
            gsend[2 + 2 * k + side, 0:16] = corner.astype(jnp.bfloat16)

    def grad_border(d, to):
        if d < 2:
            src, dst = grad.at[:, 1 + 15 * d], grad.at[:, 17 - 17 * d]
            if not to:
                dst = grad.at[:, 17 * d]
        elif d < 4:
            src = gsend.at[d - 2, 0:64]
            dst = grecv.at[(3 - d) if to else (d - 2), 0:64]
        else:
            src = gsend.at[d - 2, 0:16]
            dst = grecv.at[(opposite[d] if to else d) - 2, 0:16]
        return pltpu.make_async_remote_copy(
            src_ref=src, dst_ref=dst, send_sem=hsend.at[d], recv_sem=hrecv.at[opposite[d] if to else d],
            device_id=around[d][1], device_id_type=MESH,
        )

    for d in range(8):
        pl.when(around[d][0])(grad_border(d, True).start)
    for d in range(8):
        @pl.when(jnp.logical_not(around[d][0]))
        def _():
            if d < 2:
                grad[:, 17 * d] = jnp.zeros((4, 8, 128), jnp.bfloat16)
            elif d < 4:
                grecv[d - 2] = jnp.zeros((64, 128), jnp.bfloat16)
            else:
                grecv[d - 2, 0:16] = jnp.zeros((16, 128), jnp.bfloat16)
    for d in range(8):
        pl.when(around[d][0])(grad_border(d, False).wait_recv)

    for side in range(2):
        middle = grecv[side].astype(jnp.float32)
        top = grecv[2 + side, 0:16].astype(jnp.float32)
        bottom = grecv[4 + side, 0:16].astype(jnp.float32)
        for b in range(4):
            ghalo[side, 18 * b:18 * b + 18] = jnp.concatenate(
                [top[b:b + 1], middle[16 * b:16 * b + 16], bottom[b:b + 1]], axis=0
            )

    def shift_row(i, carry):
        b, r = i // 18, i % 18
        value = grad[b, r].astype(jnp.float32)
        before, after = ghalo[0, pl.ds(i, 1)], ghalo[1, pl.ds(i, 1)]
        shifted[0, b, r] = jnp.where(lane_row == 7, after, pltpu.roll(value, 7, 0)).astype(jnp.bfloat16)
        shifted[1, b, r] = grad[b, r]
        shifted[2, b, r] = jnp.where(lane_row == 0, before, pltpu.roll(value, 1, 0)).astype(jnp.bfloat16)
        return carry

    lax.fori_loop(0, 72, shift_row, 0)
    for tap in range(9):
        a, e = divmod(tap, 3)
        lhs[:, 128 * tap:128 * tap + 128] = shifted[e, :, 2 - a:18 - a].reshape(512, 128)

    def channels(step, carry):
        first = pl.multiple_of(step * 256, 256)
        weights = jnp.concatenate(
            [down[pl.ds(pl.multiple_of(C * tap + first, 256), 256)] for tap in range(9)], axis=1
        )
        out = lax.dot_general(lhs[...], weights, (((1,), (1,)), ((), ())), preferred_element_type=jnp.float32)
        kept = maps[1, :, 1:17, :, pl.ds(first, 256)].reshape(512, 256).astype(jnp.float32)
        result[:, pl.ds(first, 256)] = (out + kept).astype(jnp.bfloat16)
        return carry

    lax.fori_loop(0, 5, channels, 0)
    final = pltpu.make_async_copy(result, out_ref, osem)
    final.start()
    for copy, when in chunks + waits:
        if when is None:
            copy.wait_send()
        else:
            pl.when(when)(copy.wait_send)
    for n, ref in enumerate((in_ref, cot_ref)):
        for d in range(2):
            pl.when(around[d][0])(map_row(n, d, ref).wait_send)
            pl.when(around[2 + d][0])(column(n, d).wait_send)
    for d in range(8):
        pl.when(around[d][0])(grad_border(d, True).wait_send)
    final.wait()


def solution(mesh):
    dma = pltpu.SemaphoreType.DMA
    bf16, f32 = jnp.bfloat16, jnp.float32

    def shards(inputs, cotangent, w_in, w_out):
        chunks = [jnp.pad(w, (0, CHUNK * 128 - 2880)).reshape(CHUNK, 128) for w in (w_in, w_out)]
        result = pl.pallas_call(
            adapter_kernel,
            out_shape=jax.ShapeDtypeStruct((512, C), bf16),
            in_specs=[
                pl.BlockSpec(memory_space=pltpu.VMEM),
                pl.BlockSpec(memory_space=pltpu.VMEM),
                pl.BlockSpec(memory_space=pl.ANY),
                pl.BlockSpec(memory_space=pl.ANY),
            ],
            out_specs=pl.BlockSpec(memory_space=pl.ANY),
            scratch_shapes=[
                pltpu.VMEM((4, 2, CHUNK, 128), bf16),
                pltpu.VMEM((FRAME, 128), f32),
                pltpu.VMEM((2, 4, 8, 2, FRAME, 128), bf16),
                pltpu.VMEM((2, 4, 18, 8, C), bf16),
                pltpu.VMEM((2, 2, 80, C), bf16),
                pltpu.VMEM((2, 2, 80, C), bf16),
                pltpu.VMEM((2, 736, 1280), f32),
                pltpu.VMEM((2, 2, 64, 128), f32),
                pltpu.VMEM((12800, 128), bf16),
                pltpu.VMEM((11520, 128), bf16),
                pltpu.VMEM((1280, 128), f32),
                pltpu.VMEM((1280, C), bf16),
                pltpu.VMEM((4, 18, 8, 128), bf16),
                pltpu.VMEM((2, 72, 128), f32),
                pltpu.VMEM((6, 64, 128), bf16),
                pltpu.VMEM((6, 64, 128), bf16),
                pltpu.VMEM((2, 64, 128), f32),
                pltpu.VMEM((3, 4, 18, 8, 128), bf16),
                pltpu.VMEM((512, 1152), bf16),
                pltpu.VMEM((512, C), bf16),
                dma((8,)), dma((4, 2)), dma((32, 8)), dma((4, 8)), dma((4, 8)), dma((64,)), dma((4, 8, 2)),
                dma((2, 4)), dma((2, 4)), dma((8,)), dma((8,)), dma((3,)), dma,
            ],
            compiler_params=pltpu.CompilerParams(
                collective_id=0, has_side_effects=True, vmem_limit_bytes=56 << 20
            ),
        )(*chunks, inputs, cotangent)
        return result.reshape(4, 16, 8, C)

    spec = P(None, "row", "col", None)
    flat = P(("row", "col"))
    return jax.shard_map(
        shards, mesh=mesh, in_specs=(spec, spec, flat, flat), out_specs=spec, check_vma=False
    )
```

```python
import jax
import jax.numpy as jnp
from jax import lax
from jax.experimental import pallas as pl
from jax.experimental.pallas import tpu as pltpu
from jax.sharding import PartitionSpec as P

C = 1280
MESH = pl.DeviceIdType.MESH
CHUNK = 24
FRAME = 192
LAG = 12

ORDER = [
    (0, 0),
    (1, 0), (3, 0), (0, 1), (0, -1), (2, 0), (0, 2), (0, -2),
    (1, 1), (1, -1), (3, 1), (3, -1), (1, 2), (1, -2), (3, 2), (3, -2),
    (2, 1), (2, -1), (2, 2), (2, -2), (0, 3), (0, -3), (0, 4),
    (1, 3), (1, -3), (3, 3), (3, -3), (2, 3), (2, -3), (1, 4), (3, 4), (2, 4),
]


def adapter_kernel(
    win_ref, wout_ref, in_ref, cot_ref, out_ref,
    raw, flat, units, maps, edge, cols, prod, beside, down, uflat, utap, upk, grad, ghalo, gsend, grecv, gcol, shifted, lhs,
    rsend, rrecv, usend, urecv, zrecv, psend, precv, xsend, xrecv, hsend, hrecv, lsem,
):
    row, col = lax.axis_index("row"), lax.axis_index("col")
    h, x = row // 4, row % 4
    z, l, c = col // 4, (col // 2) % 2, col % 2
    y, zp = 2 * h + l, z % 2
    quarter, to_quarter = 2 * zp + l, z // 2
    both, no = jnp.logical_and, jnp.logical_not

    def at(xx, yy, zz, cc):
        return ((yy // 2) * 4 + xx, zz * 4 + (yy % 2) * 2 + cc)

    def along_x(d):
        return at((x + d) % 4, y, z, c)

    def along_y(d):
        return at(x, (y + d + 8) % 8, z, c)

    partner = at(x, y, z, 1 - c)
    carriers = [
        (kk, at(x, 2 * h + to_quarter % 2, to_quarter // 2 + 2 * k, kk),
         both(both(to_quarter // 2 + 2 * k == z, to_quarter % 2 == l), c == kk))
        for k in range(4) for kk in range(2)
    ]
    carried = [
        (i, cc, at(x, 2 * h + i % 2, 2 * quarter + i // 2, cc),
         both(both(2 * quarter + i // 2 == z, i % 2 == l), c == cc))
        for i in range(4) for cc in range(2)
    ]

    has_up, has_down, has_left, has_right = row > 0, row < 15, col > 0, col < 31
    around = [
        (has_up, (row - 1, col)), (has_down, (row + 1, col)),
        (has_left, (row, col - 1)), (has_right, (row, col + 1)),
        (both(has_up, has_left), (row - 1, col - 1)), (both(has_up, has_right), (row - 1, col + 1)),
        (both(has_down, has_left), (row + 1, col - 1)), (both(has_down, has_right), (row + 1, col + 1)),
    ]
    opposite = (1, 0, 3, 2, 7, 6, 5, 4)

    barrier = pltpu.get_barrier_semaphore()
    peers = [along_x(d) for d in (1, 2, 3)] + [along_y(d) for d in (1, -1, 2, -2)]
    peers += [at(x, y, (z + d) % 8, c) for d in (1, 7)] + [partner]
    for peer in peers:
        pl.semaphore_signal(barrier, inc=1, device_id=peer, device_id_type=MESH)
    for _, _, device, itself in carried:
        @pl.when(no(itself))
        def _():
            pl.semaphore_signal(barrier, inc=1, device_id=device, device_id_type=MESH)
    for exists, device in around:
        @pl.when(exists)
        def _():
            pl.semaphore_signal(barrier, inc=1, device_id=device, device_id_type=MESH)
    arrivals = sum(exists.astype(jnp.int32) for exists, _ in around)
    arrivals += sum(no(itself).astype(jnp.int32) for _, _, itself in carriers)
    pl.semaphore_wait(barrier, len(peers) + arrivals)

    place = 2 * zp + l
    chunks = []
    for n, (kk, device, itself) in enumerate(carriers):
        source = (win_ref, wout_ref)[kk]
        copy = pltpu.make_async_remote_copy(
            src_ref=source, dst_ref=raw.at[place, c], send_sem=rsend.at[n], recv_sem=rrecv.at[place, c],
            device_id=device, device_id_type=MESH,
        )
        pl.when(no(itself))(copy.start)
        chunks.append((copy, no(itself)))
        pl.when(itself)(pltpu.make_async_copy(source, raw.at[place, c], lsem.at[0]).start)
    local = [
        pltpu.make_async_copy(ref, maps.at[n, :, 1:17], lsem.at[1 + n]) for n, ref in enumerate((in_ref, cot_ref))
    ]
    for copy in local:
        copy.start()

    def map_row(n, d, ref):
        return pltpu.make_async_remote_copy(
            src_ref=ref.at[:, 15 * d], dst_ref=maps.at[n, :, 17 - 17 * d],
            send_sem=xsend.at[n, d], recv_sem=xrecv.at[n, opposite[d]],
            device_id=around[d][1], device_id_type=MESH,
        )

    def map_row_in(n, d, ref):
        return pltpu.make_async_remote_copy(
            src_ref=ref.at[:, 0], dst_ref=maps.at[n, :, 17 * d],
            send_sem=xsend.at[n, d], recv_sem=xrecv.at[n, d],
            device_id=around[d][1], device_id_type=MESH,
        )

    def border_rows():
        for n, ref in enumerate((in_ref, cot_ref)):
            for d in range(2):
                pl.when(around[d][0])(map_row(n, d, ref).start)

                @pl.when(jnp.logical_not(around[d][0]))
                def _():
                    maps[n, :, 17 * d] = jnp.zeros((4, 8, C), jnp.bfloat16)

    for i, cc, _, itself in carried:
        pl.when(no(itself))(pltpu.make_async_remote_copy(
            src_ref=raw.at[i, cc], dst_ref=raw.at[i, cc], send_sem=rsend.at[0], recv_sem=rrecv.at[i, cc],
            device_id=partner, device_id_type=MESH,
        ).wait_recv)
        pl.when(itself)(pltpu.make_async_copy(win_ref, raw.at[i, cc], lsem.at[0]).wait)

    lanes = lax.broadcasted_iota(jnp.int32, (23, 128), 1)
    pieces = []
    for i in range(4):
        even = raw[i, 0].astype(jnp.float32)
        odd = pltpu.roll(raw[i, 1].astype(jnp.float32), 64, 1)
        low = jnp.concatenate([even[22:23], odd[0:22]], axis=0)
        pieces.append((even[0:22], jnp.where(lanes < 64, low, odd[0:23])))
    flat[...] = jnp.zeros((FRAME, 128), jnp.float32)
    for k in range(4):
        @pl.when(quarter == k)
        def _():
            for i in range(4):
                first = 4 * k + 45 * i
                flat[first:first + 22] = pieces[i][0]
                flat[first + 22:first + 45] = pieces[i][1]
    units[c, x, y, zp] = flat[...].astype(jnp.bfloat16)

    def column(n, side):
        return pltpu.make_async_remote_copy(
            src_ref=edge.at[n, side], dst_ref=cols.at[n, 1 - side],
            send_sem=xsend.at[n, 2 + side], recv_sem=xrecv.at[n, 3 - side],
            device_id=around[2 + side][1], device_id_type=MESH,
        )

    def column_in(n, side):
        return pltpu.make_async_remote_copy(
            src_ref=edge.at[n, side], dst_ref=cols.at[n, side],
            send_sem=xsend.at[n, 2 + side], recv_sem=xrecv.at[n, 2 + side],
            device_id=around[2 + side][1], device_id_type=MESH,
        )

    def border_columns():
        wanted = lax.broadcasted_iota(jnp.int32, (160, 576), 0)
        wanted = jnp.where(wanted < 80, wanted * 8, (wanted - 80) * 8 + 7)
        pick = jnp.where(lax.broadcasted_iota(jnp.int32, (160, 576), 1) == wanted, 1.0, 0.0).astype(jnp.bfloat16)
        for n, ref in enumerate((in_ref, cot_ref)):
            local[n].wait()
            for d in range(2):
                pl.when(around[d][0])(map_row_in(n, d, ref).wait_recv)
            picked = jnp.dot(pick, maps[n].reshape(576, C), preferred_element_type=jnp.float32)
            edge[n] = picked.astype(jnp.bfloat16).reshape(2, 80, C)

    def border_sends():
        for n in range(2):
            for side in range(2):
                pl.when(around[2 + side][0])(column(n, side).start)

                @pl.when(jnp.logical_not(around[2 + side][0]))
                def _():
                    cols[n, side] = jnp.zeros((80, C), jnp.bfloat16)

    waits = []

    def send(unit, device, sends, receives, when):
        copy = pltpu.make_async_remote_copy(
            src_ref=unit, dst_ref=unit, send_sem=sends, recv_sem=receives,
            device_id=device, device_id_type=MESH,
        )
        if when is None:
            copy.start()
        else:
            pl.when(when)(copy.start)
        waits.append((copy, when))

    def arrived(unit, receives):
        pltpu.make_async_remote_copy(
            src_ref=unit, dst_ref=unit, send_sem=psend.at[0], recv_sem=receives,
            device_id=partner, device_id_type=MESH,
        ).wait_recv()

    def share(n, xx, yy, parity):
        send(units.at[c, xx, yy, parity], partner, psend.at[n], precv.at[xx, yy, parity], None)

    def from_z(n):
        dx, dy = ORDER[n]
        xx, yy = (x + dx) % 4, (y + dy + 8) % 8
        arrived(units.at[c, xx, yy, 1 - zp], zrecv.at[xx, yy])
        share(32 + n, xx, yy, 1 - zp)

    first, second = c == 0, c == 1
    for n, (dx, dy) in enumerate(ORDER):
        xx, yy = (x + dx) % 4, (y + dy + 8) % 8
        parity = (xx + yy) % 2
        unit = units.at[c, xx, yy, zp]
        if n:
            arrived(unit, urecv.at[xx, yy])
        steps = {0: (1, -1, 2, -2), -2: (1, 2), 2: (-1, -2)}.get(dy, ())
        for k, step in enumerate(steps):
            when = None if dx == 0 else first
            if dy and abs(step) == 2:
                chosen = parity == (0 if step > 0 else 1)
                when = chosen if when is None else both(when, chosen)
            send(unit, along_y(step), usend.at[n, k], urecv.at[xx, yy], when)
        if dx == 0:
            for k, step in enumerate((1, 3, 2)):
                send(unit, along_x(step), usend.at[n, 4 + k], urecv.at[xx, yy], None if dy == 0 else second)
        send(unit, at(x, y, (z + 1 + 6 * parity) % 8, c), usend.at[n, 7], zrecv.at[xx, yy], None)
        share(n, xx, yy, zp)
        if n == 0:
            border_rows()
        if n == 10:
            border_columns()
        if n == 20:
            border_sends()
        if n >= LAG:
            from_z(n - LAG)
    for n in range(32 - LAG, 32):
        from_z(n)
    for xx in range(4):
        for yy in range(8):
            for parity in range(2):
                arrived(units.at[1 - c, xx, yy, parity], precv.at[xx, yy, parity])

    frame_row = lax.broadcasted_iota(jnp.int32, (16, 128), 0)
    for k, whole in enumerate((down, uflat)):
        for g in range(16):
            frames = [units.at[k, g % 4, 2 * (g // 4) + q % 2, q // 2] for q in range(4)]
            for q in range(4):
                start = 720 * g + 176 * q
                last = FRAME if q == 3 else 176
                begin = 16 if q else 0
                whole[start + begin:start + last] = frames[q][begin:last]
                if q:
                    seam = jnp.where(
                        frame_row < 4 * q, frames[q - 1][176:192].astype(jnp.float32),
                        frames[q][0:16].astype(jnp.float32),
                    )
                    whole[start:start + 16] = seam.astype(jnp.bfloat16)
    down[11520:12800] = jnp.zeros((1280, 128), jnp.bfloat16)

    def up_tap(tap, carry):
        utap[...] = uflat[pl.ds(pl.multiple_of(tap * 1280, 1280), 1280)].astype(jnp.float32)
        for j in range(10):
            rows = utap[pl.ds(j, 128, stride=10), :].astype(jnp.bfloat16)
            upk[pl.ds(pl.multiple_of((8 - tap) * 128, 128), 128), 128 * j:128 * j + 128] = rows
        return carry

    lax.fori_loop(0, 9, up_tap, 0)
    upk[1152:1280] = jnp.zeros((128, C), jnp.bfloat16)
    for n in range(2):
        for side in range(2):
            pl.when(around[2 + side][0])(column_in(n, side).wait_recv)

    pixels = [
        jnp.concatenate([maps[n].reshape(576, C), cols[n].reshape(160, C)], axis=0) for n in range(2)
    ]

    def two_taps(step, carry):
        first = pl.multiple_of(step * 2560, 2560)
        two = jnp.concatenate([down[pl.ds(first, C)], down[pl.ds(first + C, C)]], axis=1)
        out = pl.ds(pl.multiple_of(step * 256, 256), 256)
        prod[0, :, out] = jnp.dot(pixels[0], two, preferred_element_type=jnp.float32)
        rows = upk[pl.ds(pl.multiple_of(step * 256, 256), 256)]
        prod[1, :, out] = lax.dot_general(
            pixels[1], rows, (((1,), (1,)), ((), ())), preferred_element_type=jnp.float32
        )
        return carry

    lax.fori_loop(0, 5, two_taps, 0)

    lane_row = lax.broadcasted_iota(jnp.int32, (8, 128), 0)
    for n in range(2):
        for side in range(2):
            three = [
                prod[n, 576 + 80 * side:656 + 80 * side, 128 * (3 * a + 2 * side):128 * (3 * a + 2 * side) + 128]
                for a in range(3)
            ]
            for b in range(4):
                terms = [three[a][18 * b + a:18 * b + a + 16] for a in range(3)]
                beside[n, side, 16 * b:16 * b + 16] = terms[0] + terms[1] + terms[2]

    def pixel_row(i, carry):
        b, r = i // 16, i % 16
        sums = []
        for n in range(2):
            three = []
            for e in range(3):
                terms = [
                    prod[n, pl.ds(pl.multiple_of((b * 18 + r + a) * 8, 8), 8), 128 * (3 * a + e):128 * (3 * a + e) + 128]
                    for a in range(3)
                ]
                three.append(terms[0] + terms[1] + terms[2])
            sides = [beside[n, side, pl.ds(i, 1)] for side in range(2)]
            sums.append(
                jnp.where(lane_row == 0, sides[0], pltpu.roll(three[0], 1, 0))
                + three[1]
                + jnp.where(lane_row == 7, sides[1], pltpu.roll(three[2], 7, 0))
            )
        pre, back = sums
        s = jax.nn.sigmoid(pre)
        value = (back * (s * (1.0 + pre * (1.0 - s)))).astype(jnp.bfloat16)
        grad[b, 1 + r] = value
        value = value.astype(jnp.float32)
        gcol[0, pl.ds(i, 1)] = value[0:1]
        gcol[1, pl.ds(i, 1)] = value[7:8]
        return carry

    lax.fori_loop(0, 64, pixel_row, 0)

    for side in range(2):
        gsend[side] = gcol[side, 0:64].astype(jnp.bfloat16)
        for k in range(2):
            corner = [gcol[side, 16 * b + 15 * k:16 * b + 15 * k + 1] for b in range(4)]
            corner = jnp.concatenate(corner + [jnp.zeros((12, 128), jnp.float32)], axis=0)
            gsend[2 + 2 * k + side, 0:16] = corner.astype(jnp.bfloat16)

    def grad_border(d, to):
        if d < 2:
            src, dst = grad.at[:, 1 + 15 * d], grad.at[:, 17 - 17 * d]
            if not to:
                dst = grad.at[:, 17 * d]
        elif d < 4:
            src = gsend.at[d - 2, 0:64]
            dst = grecv.at[(3 - d) if to else (d - 2), 0:64]
        else:
            src = gsend.at[d - 2, 0:16]
            dst = grecv.at[(opposite[d] if to else d) - 2, 0:16]
        return pltpu.make_async_remote_copy(
            src_ref=src, dst_ref=dst, send_sem=hsend.at[d], recv_sem=hrecv.at[opposite[d] if to else d],
            device_id=around[d][1], device_id_type=MESH,
        )

    for d in range(8):
        pl.when(around[d][0])(grad_border(d, True).start)
    for d in range(8):
        @pl.when(jnp.logical_not(around[d][0]))
        def _():
            if d < 2:
                grad[:, 17 * d] = jnp.zeros((4, 8, 128), jnp.bfloat16)
            elif d < 4:
                grecv[d - 2] = jnp.zeros((64, 128), jnp.bfloat16)
            else:
                grecv[d - 2, 0:16] = jnp.zeros((16, 128), jnp.bfloat16)
    for d in range(8):
        pl.when(around[d][0])(grad_border(d, False).wait_recv)

    for side in range(2):
        middle = grecv[side].astype(jnp.float32)
        top = grecv[2 + side, 0:16].astype(jnp.float32)
        bottom = grecv[4 + side, 0:16].astype(jnp.float32)
        for b in range(4):
            ghalo[side, 18 * b:18 * b + 18] = jnp.concatenate(
                [top[b:b + 1], middle[16 * b:16 * b + 16], bottom[b:b + 1]], axis=0
            )

    def shift_row(i, carry):
        b, r = i // 18, i % 18
        value = grad[b, r].astype(jnp.float32)
        before, after = ghalo[0, pl.ds(i, 1)], ghalo[1, pl.ds(i, 1)]
        shifted[0, b, r] = jnp.where(lane_row == 7, after, pltpu.roll(value, 7, 0)).astype(jnp.bfloat16)
        shifted[1, b, r] = grad[b, r]
        shifted[2, b, r] = jnp.where(lane_row == 0, before, pltpu.roll(value, 1, 0)).astype(jnp.bfloat16)
        return carry

    lax.fori_loop(0, 72, shift_row, 0)
    for tap in range(9):
        a, e = divmod(tap, 3)
        lhs[:, 128 * tap:128 * tap + 128] = shifted[e, :, 2 - a:18 - a].reshape(512, 128)

    def channels(step, carry):
        first = pl.multiple_of(step * 256, 256)
        weights = jnp.concatenate(
            [down[pl.ds(pl.multiple_of(C * tap + first, 256), 256)] for tap in range(9)], axis=1
        )
        out = lax.dot_general(lhs[...], weights, (((1,), (1,)), ((), ())), preferred_element_type=jnp.float32)
        kept = maps[1, :, 1:17, :, pl.ds(first, 256)].reshape(512, 256).astype(jnp.float32)
        out_ref[:, pl.ds(first, 256)] = (out + kept).astype(jnp.bfloat16)
        return carry

    lax.fori_loop(0, 5, channels, 0)
    for copy, when in chunks + waits:
        if when is None:
            copy.wait_send()
        else:
            pl.when(when)(copy.wait_send)
    for n, ref in enumerate((in_ref, cot_ref)):
        for d in range(2):
            pl.when(around[d][0])(map_row(n, d, ref).wait_send)
            pl.when(around[2 + d][0])(column(n, d).wait_send)
    for d in range(8):
        pl.when(around[d][0])(grad_border(d, True).wait_send)


def solution(mesh):
    dma = pltpu.SemaphoreType.DMA
    bf16, f32 = jnp.bfloat16, jnp.float32

    def shards(inputs, cotangent, w_in, w_out):
        chunks = [jnp.pad(w, (0, CHUNK * 128 - 2880)).reshape(CHUNK, 128) for w in (w_in, w_out)]
        result = pl.pallas_call(
            adapter_kernel,
            out_shape=jax.ShapeDtypeStruct((512, C), bf16),
            in_specs=[
                pl.BlockSpec(memory_space=pltpu.VMEM),
                pl.BlockSpec(memory_space=pltpu.VMEM),
                pl.BlockSpec(memory_space=pl.ANY),
                pl.BlockSpec(memory_space=pl.ANY),
            ],
            out_specs=pl.BlockSpec(memory_space=pltpu.VMEM),
            scratch_shapes=[
                pltpu.VMEM((4, 2, CHUNK, 128), bf16),
                pltpu.VMEM((FRAME, 128), f32),
                pltpu.VMEM((2, 4, 8, 2, FRAME, 128), bf16),
                pltpu.VMEM((2, 4, 18, 8, C), bf16),
                pltpu.VMEM((2, 2, 80, C), bf16),
                pltpu.VMEM((2, 2, 80, C), bf16),
                pltpu.VMEM((2, 736, 1280), f32),
                pltpu.VMEM((2, 2, 64, 128), f32),
                pltpu.VMEM((12800, 128), bf16),
                pltpu.VMEM((11520, 128), bf16),
                pltpu.VMEM((1280, 128), f32),
                pltpu.VMEM((1280, C), bf16),
                pltpu.VMEM((4, 18, 8, 128), bf16),
                pltpu.VMEM((2, 72, 128), f32),
                pltpu.VMEM((6, 64, 128), bf16),
                pltpu.VMEM((6, 64, 128), bf16),
                pltpu.VMEM((2, 64, 128), f32),
                pltpu.VMEM((3, 4, 18, 8, 128), bf16),
                pltpu.VMEM((512, 1152), bf16),
                dma((8,)), dma((4, 2)), dma((32, 8)), dma((4, 8)), dma((4, 8)), dma((64,)), dma((4, 8, 2)),
                dma((2, 4)), dma((2, 4)), dma((8,)), dma((8,)), dma((3,)),
            ],
            compiler_params=pltpu.CompilerParams(
                collective_id=0, has_side_effects=True, vmem_limit_bytes=44 << 20
            ),
        )(*chunks, inputs, cotangent)
        return result.reshape(4, 16, 8, C)

    spec = P(None, "row", "col", None)
    flat = P(("row", "col"))
    return jax.shard_map(
        shards, mesh=mesh, in_specs=(spec, spec, flat, flat), out_specs=spec, check_vma=False
    )
```

```python
import jax
import jax.numpy as jnp
from jax import lax
from jax.experimental import pallas as pl
from jax.experimental.pallas import tpu as pltpu
from jax.sharding import PartitionSpec as P

C = 1280
MESH = pl.DeviceIdType.MESH
CHUNK = 24
FRAME = 192
LAG = 12

ORDER = [
    (0, 0),
    (1, 0), (3, 0), (0, 1), (0, -1), (2, 0), (0, 2), (0, -2),
    (1, 1), (1, -1), (3, 1), (3, -1), (1, 2), (1, -2), (3, 2), (3, -2),
    (2, 1), (2, -1), (2, 2), (2, -2), (0, 3), (0, -3), (0, 4),
    (1, 3), (1, -3), (3, 3), (3, -3), (2, 3), (2, -3), (1, 4), (3, 4), (2, 4),
]


def adapter_kernel(
    win_ref, wout_ref, in_ref, cot_ref, out_ref,
    raw, flat, units, maps, edge, cols, prod, beside, down, uflat, utap, upk, grad, ghalo, gsend, grecv, gcol, shifted, lhs,
    rsend, rrecv, usend, urecv, zrecv, psend, precv, xsend, xrecv, hsend, hrecv, lsem,
):
    row, col = lax.axis_index("row"), lax.axis_index("col")
    h, x = row // 4, row % 4
    z, l, c = col // 4, (col // 2) % 2, col % 2
    y, zp = 2 * h + l, z % 2
    quarter, to_quarter = 2 * zp + l, z // 2
    both, no = jnp.logical_and, jnp.logical_not

    def at(xx, yy, zz, cc):
        return ((yy // 2) * 4 + xx, zz * 4 + (yy % 2) * 2 + cc)

    def along_x(d):
        return at((x + d) % 4, y, z, c)

    def along_y(d):
        return at(x, (y + d + 8) % 8, z, c)

    partner = at(x, y, z, 1 - c)
    carriers = [
        (kk, at(x, 2 * h + to_quarter % 2, to_quarter // 2 + 2 * k, kk),
         both(both(to_quarter // 2 + 2 * k == z, to_quarter % 2 == l), c == kk))
        for k in range(4) for kk in range(2)
    ]
    carried = [
        (i, cc, at(x, 2 * h + i % 2, 2 * quarter + i // 2, cc),
         both(both(2 * quarter + i // 2 == z, i % 2 == l), c == cc))
        for i in range(4) for cc in range(2)
    ]

    has_up, has_down, has_left, has_right = row > 0, row < 15, col > 0, col < 31
    around = [
        (has_up, (row - 1, col)), (has_down, (row + 1, col)),
        (has_left, (row, col - 1)), (has_right, (row, col + 1)),
        (both(has_up, has_left), (row - 1, col - 1)), (both(has_up, has_right), (row - 1, col + 1)),
        (both(has_down, has_left), (row + 1, col - 1)), (both(has_down, has_right), (row + 1, col + 1)),
    ]
    opposite = (1, 0, 3, 2, 7, 6, 5, 4)

    barrier = pltpu.get_barrier_semaphore()
    peers = [along_x(d) for d in (1, 2, 3)] + [along_y(d) for d in (1, -1, 2, -2)]
    peers += [at(x, y, (z + d) % 8, c) for d in (1, 7)] + [partner]
    for peer in peers:
        pl.semaphore_signal(barrier, inc=1, device_id=peer, device_id_type=MESH)
    for _, _, device, itself in carried:
        @pl.when(no(itself))
        def _():
            pl.semaphore_signal(barrier, inc=1, device_id=device, device_id_type=MESH)
    for exists, device in around:
        @pl.when(exists)
        def _():
            pl.semaphore_signal(barrier, inc=1, device_id=device, device_id_type=MESH)
    arrivals = sum(exists.astype(jnp.int32) for exists, _ in around)
    arrivals += sum(no(itself).astype(jnp.int32) for _, _, itself in carriers)
    pl.semaphore_wait(barrier, len(peers) + arrivals)

    place = 2 * zp + l
    chunks = []
    for n, (kk, device, itself) in enumerate(carriers):
        source = (win_ref, wout_ref)[kk]
        copy = pltpu.make_async_remote_copy(
            src_ref=source, dst_ref=raw.at[place, c], send_sem=rsend.at[n], recv_sem=rrecv.at[place, c],
            device_id=device, device_id_type=MESH,
        )
        pl.when(no(itself))(copy.start)
        chunks.append((copy, no(itself)))
        pl.when(itself)(pltpu.make_async_copy(source, raw.at[place, c], lsem.at[0]).start)
    local = [
        pltpu.make_async_copy(ref, maps.at[n, :, 1:17], lsem.at[1 + n]) for n, ref in enumerate((in_ref, cot_ref))
    ]
    for copy in local:
        copy.start()

    def map_row(n, d, ref):
        return pltpu.make_async_remote_copy(
            src_ref=ref.at[:, 15 * d], dst_ref=maps.at[n, :, 17 - 17 * d],
            send_sem=xsend.at[n, d], recv_sem=xrecv.at[n, opposite[d]],
            device_id=around[d][1], device_id_type=MESH,
        )

    def map_row_in(n, d, ref):
        return pltpu.make_async_remote_copy(
            src_ref=ref.at[:, 0], dst_ref=maps.at[n, :, 17 * d],
            send_sem=xsend.at[n, d], recv_sem=xrecv.at[n, d],
            device_id=around[d][1], device_id_type=MESH,
        )

    def border_rows():
        for n, ref in enumerate((in_ref, cot_ref)):
            for d in range(2):
                pl.when(around[d][0])(map_row(n, d, ref).start)

                @pl.when(jnp.logical_not(around[d][0]))
                def _():
                    maps[n, :, 17 * d] = jnp.zeros((4, 8, C), jnp.bfloat16)

    border_rows()
    for i, cc, _, itself in carried:
        pl.when(no(itself))(pltpu.make_async_remote_copy(
            src_ref=raw.at[i, cc], dst_ref=raw.at[i, cc], send_sem=rsend.at[0], recv_sem=rrecv.at[i, cc],
            device_id=partner, device_id_type=MESH,
        ).wait_recv)
        pl.when(itself)(pltpu.make_async_copy(win_ref, raw.at[i, cc], lsem.at[0]).wait)

    lanes = lax.broadcasted_iota(jnp.int32, (23, 128), 1)
    pieces = []
    for i in range(4):
        even = raw[i, 0].astype(jnp.float32)
        odd = pltpu.roll(raw[i, 1].astype(jnp.float32), 64, 1)
        low = jnp.concatenate([even[22:23], odd[0:22]], axis=0)
        pieces.append((even[0:22], jnp.where(lanes < 64, low, odd[0:23])))
    flat[...] = jnp.zeros((FRAME, 128), jnp.float32)
    for k in range(4):
        @pl.when(quarter == k)
        def _():
            for i in range(4):
                first = 4 * k + 45 * i
                flat[first:first + 22] = pieces[i][0]
                flat[first + 22:first + 45] = pieces[i][1]
    units[c, x, y, zp] = flat[...].astype(jnp.bfloat16)

    def column(n, side):
        return pltpu.make_async_remote_copy(
            src_ref=edge.at[n, side], dst_ref=cols.at[n, 1 - side],
            send_sem=xsend.at[n, 2 + side], recv_sem=xrecv.at[n, 3 - side],
            device_id=around[2 + side][1], device_id_type=MESH,
        )

    def column_in(n, side):
        return pltpu.make_async_remote_copy(
            src_ref=edge.at[n, side], dst_ref=cols.at[n, side],
            send_sem=xsend.at[n, 2 + side], recv_sem=xrecv.at[n, 2 + side],
            device_id=around[2 + side][1], device_id_type=MESH,
        )

    def border_columns():
        wanted = lax.broadcasted_iota(jnp.int32, (160, 576), 0)
        wanted = jnp.where(wanted < 80, wanted * 8, (wanted - 80) * 8 + 7)
        pick = jnp.where(lax.broadcasted_iota(jnp.int32, (160, 576), 1) == wanted, 1.0, 0.0).astype(jnp.bfloat16)
        for n, ref in enumerate((in_ref, cot_ref)):
            local[n].wait()
            for d in range(2):
                pl.when(around[d][0])(map_row_in(n, d, ref).wait_recv)
            picked = jnp.dot(pick, maps[n].reshape(576, C), preferred_element_type=jnp.float32)
            edge[n] = picked.astype(jnp.bfloat16).reshape(2, 80, C)

    def border_sends():
        for n in range(2):
            for side in range(2):
                pl.when(around[2 + side][0])(column(n, side).start)

                @pl.when(jnp.logical_not(around[2 + side][0]))
                def _():
                    cols[n, side] = jnp.zeros((80, C), jnp.bfloat16)

    waits = []

    def send(unit, device, sends, receives, when):
        copy = pltpu.make_async_remote_copy(
            src_ref=unit, dst_ref=unit, send_sem=sends, recv_sem=receives,
            device_id=device, device_id_type=MESH,
        )
        if when is None:
            copy.start()
        else:
            pl.when(when)(copy.start)
        waits.append((copy, when))

    def arrived(unit, receives):
        pltpu.make_async_remote_copy(
            src_ref=unit, dst_ref=unit, send_sem=psend.at[0], recv_sem=receives,
            device_id=partner, device_id_type=MESH,
        ).wait_recv()

    def share(n, xx, yy, parity):
        send(units.at[c, xx, yy, parity], partner, psend.at[n], precv.at[xx, yy, parity], None)

    def from_z(n):
        dx, dy = ORDER[n]
        xx, yy = (x + dx) % 4, (y + dy + 8) % 8
        arrived(units.at[c, xx, yy, 1 - zp], zrecv.at[xx, yy])
        share(32 + n, xx, yy, 1 - zp)

    first, second = c == 0, c == 1
    for n, (dx, dy) in enumerate(ORDER):
        xx, yy = (x + dx) % 4, (y + dy + 8) % 8
        parity = (xx + yy) % 2
        unit = units.at[c, xx, yy, zp]
        if n:
            arrived(unit, urecv.at[xx, yy])
        steps = {0: (1, -1, 2, -2), -2: (1, 2), 2: (-1, -2)}.get(dy, ())
        for k, step in enumerate(steps):
            when = None if dx == 0 else first
            if dy and abs(step) == 2:
                chosen = parity == (0 if step > 0 else 1)
                when = chosen if when is None else both(when, chosen)
            send(unit, along_y(step), usend.at[n, k], urecv.at[xx, yy], when)
        if dx == 0:
            for k, step in enumerate((1, 3, 2)):
                send(unit, along_x(step), usend.at[n, 4 + k], urecv.at[xx, yy], None if dy == 0 else second)
        send(unit, at(x, y, (z + 1 + 6 * parity) % 8, c), usend.at[n, 7], zrecv.at[xx, yy], None)
        share(n, xx, yy, zp)
        if n == 0:
            border_columns()
        if n == 20:
            border_sends()
        if n >= LAG:
            from_z(n - LAG)
    for n in range(32 - LAG, 32):
        from_z(n)
    for xx in range(4):
        for yy in range(8):
            for parity in range(2):
                arrived(units.at[1 - c, xx, yy, parity], precv.at[xx, yy, parity])

    frame_row = lax.broadcasted_iota(jnp.int32, (16, 128), 0)
    for k, whole in enumerate((down, uflat)):
        for g in range(16):
            frames = [units.at[k, g % 4, 2 * (g // 4) + q % 2, q // 2] for q in range(4)]
            for q in range(4):
                start = 720 * g + 176 * q
                last = FRAME if q == 3 else 176
                begin = 16 if q else 0
                whole[start + begin:start + last] = frames[q][begin:last]
                if q:
                    seam = jnp.where(
                        frame_row < 4 * q, frames[q - 1][176:192].astype(jnp.float32),
                        frames[q][0:16].astype(jnp.float32),
                    )
                    whole[start:start + 16] = seam.astype(jnp.bfloat16)
    down[11520:12800] = jnp.zeros((1280, 128), jnp.bfloat16)

    def up_tap(tap, carry):
        utap[...] = uflat[pl.ds(pl.multiple_of(tap * 1280, 1280), 1280)].astype(jnp.float32)
        for j in range(10):
            rows = utap[pl.ds(j, 128, stride=10), :].astype(jnp.bfloat16)
            upk[pl.ds(pl.multiple_of((8 - tap) * 128, 128), 128), 128 * j:128 * j + 128] = rows
        return carry

    lax.fori_loop(0, 9, up_tap, 0)
    upk[1152:1280] = jnp.zeros((128, C), jnp.bfloat16)
    for n in range(2):
        for side in range(2):
            pl.when(around[2 + side][0])(column_in(n, side).wait_recv)

    pixels = [
        jnp.concatenate([maps[n].reshape(576, C), cols[n].reshape(160, C)], axis=0) for n in range(2)
    ]

    def two_taps(step, carry):
        first = pl.multiple_of(step * 2560, 2560)
        two = jnp.concatenate([down[pl.ds(first, C)], down[pl.ds(first + C, C)]], axis=1)
        out = pl.ds(pl.multiple_of(step * 256, 256), 256)
        prod[0, :, out] = jnp.dot(pixels[0], two, preferred_element_type=jnp.float32)
        rows = upk[pl.ds(pl.multiple_of(step * 256, 256), 256)]
        prod[1, :, out] = lax.dot_general(
            pixels[1], rows, (((1,), (1,)), ((), ())), preferred_element_type=jnp.float32
        )
        return carry

    lax.fori_loop(0, 5, two_taps, 0)

    lane_row = lax.broadcasted_iota(jnp.int32, (8, 128), 0)
    for n in range(2):
        for side in range(2):
            three = [
                prod[n, 576 + 80 * side:656 + 80 * side, 128 * (3 * a + 2 * side):128 * (3 * a + 2 * side) + 128]
                for a in range(3)
            ]
            for b in range(4):
                terms = [three[a][18 * b + a:18 * b + a + 16] for a in range(3)]
                beside[n, side, 16 * b:16 * b + 16] = terms[0] + terms[1] + terms[2]

    def pixel_row(i, carry):
        b, r = i // 16, i % 16
        sums = []
        for n in range(2):
            three = []
            for e in range(3):
                terms = [
                    prod[n, pl.ds(pl.multiple_of((b * 18 + r + a) * 8, 8), 8), 128 * (3 * a + e):128 * (3 * a + e) + 128]
                    for a in range(3)
                ]
                three.append(terms[0] + terms[1] + terms[2])
            sides = [beside[n, side, pl.ds(i, 1)] for side in range(2)]
            sums.append(
                jnp.where(lane_row == 0, sides[0], pltpu.roll(three[0], 1, 0))
                + three[1]
                + jnp.where(lane_row == 7, sides[1], pltpu.roll(three[2], 7, 0))
            )
        pre, back = sums
        s = jax.nn.sigmoid(pre)
        value = (back * (s * (1.0 + pre * (1.0 - s)))).astype(jnp.bfloat16)
        grad[b, 1 + r] = value
        value = value.astype(jnp.float32)
        gcol[0, pl.ds(i, 1)] = value[0:1]
        gcol[1, pl.ds(i, 1)] = value[7:8]
        return carry

    lax.fori_loop(0, 8, lambda k, carry: pixel_row((k // 2) * 16 + (k % 2) * 15, carry), 0)

    for side in range(2):
        for k in range(2):
            corner = [gcol[side, 16 * b + 15 * k:16 * b + 15 * k + 1] for b in range(4)]
            corner = jnp.concatenate(corner + [jnp.zeros((12, 128), jnp.float32)], axis=0)
            gsend[2 + 2 * k + side, 0:16] = corner.astype(jnp.bfloat16)

    def grad_border(d, to):
        if d < 2:
            src, dst = grad.at[:, 1 + 15 * d], grad.at[:, 17 - 17 * d]
            if not to:
                dst = grad.at[:, 17 * d]
        elif d < 4:
            src = gsend.at[d - 2, 0:64]
            dst = grecv.at[(3 - d) if to else (d - 2), 0:64]
        else:
            src = gsend.at[d - 2, 0:16]
            dst = grecv.at[(opposite[d] if to else d) - 2, 0:16]
        return pltpu.make_async_remote_copy(
            src_ref=src, dst_ref=dst, send_sem=hsend.at[d], recv_sem=hrecv.at[opposite[d] if to else d],
            device_id=around[d][1], device_id_type=MESH,
        )

    for d in (4, 5, 6, 7, 0, 1):
        pl.when(around[d][0])(grad_border(d, True).start)
    lax.fori_loop(0, 56, lambda k, carry: pixel_row((k // 14) * 16 + 1 + k % 14, carry), 0)
    for side in range(2):
        gsend[side] = gcol[side, 0:64].astype(jnp.bfloat16)
        pl.when(around[2 + side][0])(grad_border(2 + side, True).start)
    for d in range(8):
        @pl.when(jnp.logical_not(around[d][0]))
        def _():
            if d < 2:
                grad[:, 17 * d] = jnp.zeros((4, 8, 128), jnp.bfloat16)
            elif d < 4:
                grecv[d - 2] = jnp.zeros((64, 128), jnp.bfloat16)
            else:
                grecv[d - 2, 0:16] = jnp.zeros((16, 128), jnp.bfloat16)
    for d in range(8):
        pl.when(around[d][0])(grad_border(d, False).wait_recv)

    for side in range(2):
        middle = grecv[side].astype(jnp.float32)
        top = grecv[2 + side, 0:16].astype(jnp.float32)
        bottom = grecv[4 + side, 0:16].astype(jnp.float32)
        for b in range(4):
            ghalo[side, 18 * b:18 * b + 18] = jnp.concatenate(
                [top[b:b + 1], middle[16 * b:16 * b + 16], bottom[b:b + 1]], axis=0
            )

    def shift_row(i, carry):
        b, r = i // 18, i % 18
        value = grad[b, r].astype(jnp.float32)
        before, after = ghalo[0, pl.ds(i, 1)], ghalo[1, pl.ds(i, 1)]
        shifted[0, b, r] = jnp.where(lane_row == 7, after, pltpu.roll(value, 7, 0)).astype(jnp.bfloat16)
        shifted[1, b, r] = grad[b, r]
        shifted[2, b, r] = jnp.where(lane_row == 0, before, pltpu.roll(value, 1, 0)).astype(jnp.bfloat16)
        return carry

    lax.fori_loop(0, 72, shift_row, 0)
    for tap in range(9):
        a, e = divmod(tap, 3)
        lhs[:, 128 * tap:128 * tap + 128] = shifted[e, :, 2 - a:18 - a].reshape(512, 128)

    def channels(step, carry):
        first = pl.multiple_of(step * 256, 256)
        weights = jnp.concatenate(
            [down[pl.ds(pl.multiple_of(C * tap + first, 256), 256)] for tap in range(9)], axis=1
        )
        out = lax.dot_general(lhs[...], weights, (((1,), (1,)), ((), ())), preferred_element_type=jnp.float32)
        kept = maps[1, :, 1:17, :, pl.ds(first, 256)].reshape(512, 256).astype(jnp.float32)
        out_ref[:, pl.ds(first, 256)] = (out + kept).astype(jnp.bfloat16)
        return carry

    lax.fori_loop(0, 5, channels, 0)
    for copy, when in chunks + waits:
        if when is None:
            copy.wait_send()
        else:
            pl.when(when)(copy.wait_send)
    for n, ref in enumerate((in_ref, cot_ref)):
        for d in range(2):
            pl.when(around[d][0])(map_row(n, d, ref).wait_send)
            pl.when(around[2 + d][0])(column(n, d).wait_send)
    for d in range(8):
        pl.when(around[d][0])(grad_border(d, True).wait_send)


def solution(mesh):
    dma = pltpu.SemaphoreType.DMA
    bf16, f32 = jnp.bfloat16, jnp.float32

    def shards(inputs, cotangent, w_in, w_out):
        chunks = [jnp.pad(w, (0, CHUNK * 128 - 2880)).reshape(CHUNK, 128) for w in (w_in, w_out)]
        result = pl.pallas_call(
            adapter_kernel,
            out_shape=jax.ShapeDtypeStruct((512, C), bf16),
            in_specs=[
                pl.BlockSpec(memory_space=pltpu.VMEM),
                pl.BlockSpec(memory_space=pltpu.VMEM),
                pl.BlockSpec(memory_space=pltpu.HBM),
                pl.BlockSpec(memory_space=pltpu.HBM),
            ],
            out_specs=pl.BlockSpec(memory_space=pltpu.VMEM),
            scratch_shapes=[
                pltpu.VMEM((4, 2, CHUNK, 128), bf16),
                pltpu.VMEM((FRAME, 128), f32),
                pltpu.VMEM((2, 4, 8, 2, FRAME, 128), bf16),
                pltpu.VMEM((2, 4, 18, 8, C), bf16),
                pltpu.VMEM((2, 2, 80, C), bf16),
                pltpu.VMEM((2, 2, 80, C), bf16),
                pltpu.VMEM((2, 736, 1280), f32),
                pltpu.VMEM((2, 2, 64, 128), f32),
                pltpu.VMEM((12800, 128), bf16),
                pltpu.VMEM((11520, 128), bf16),
                pltpu.VMEM((1280, 128), f32),
                pltpu.VMEM((1280, C), bf16),
                pltpu.VMEM((4, 18, 8, 128), bf16),
                pltpu.VMEM((2, 72, 128), f32),
                pltpu.VMEM((6, 64, 128), bf16),
                pltpu.VMEM((6, 64, 128), bf16),
                pltpu.VMEM((2, 64, 128), f32),
                pltpu.VMEM((3, 4, 18, 8, 128), bf16),
                pltpu.VMEM((512, 1152), bf16),
                dma((8,)), dma((4, 2)), dma((32, 8)), dma((4, 8)), dma((4, 8)), dma((64,)), dma((4, 8, 2)),
                dma((2, 4)), dma((2, 4)), dma((8,)), dma((8,)), dma((3,)),
            ],
            compiler_params=pltpu.CompilerParams(
                collective_id=0, has_side_effects=True, vmem_limit_bytes=44 << 20
            ),
        )(*chunks, inputs, cotangent)
        return result.reshape(4, 16, 8, C)

    spec = P(None, "row", "col", None)
    flat = P(("row", "col"))
    return jax.shard_map(
        shards, mesh=mesh, in_specs=(spec, spec, flat, flat), out_specs=spec, check_vma=False
    )
```

```python
import jax
import jax.numpy as jnp
from jax import lax
from jax.experimental import pallas as pl
from jax.experimental.pallas import tpu as pltpu
from jax.sharding import PartitionSpec as P

C = 1280
MESH = pl.DeviceIdType.MESH
CHUNK = 24
FRAME = 192
LAG = 12

ORDER = [
    (0, 0),
    (1, 0), (3, 0), (0, 1), (0, -1), (2, 0), (0, 2), (0, -2),
    (1, 1), (1, -1), (3, 1), (3, -1), (1, 2), (1, -2), (3, 2), (3, -2),
    (2, 1), (2, -1), (2, 2), (2, -2), (0, 3), (0, -3), (0, 4),
    (1, 3), (1, -3), (3, 3), (3, -3), (2, 3), (2, -3), (1, 4), (3, 4), (2, 4),
]


def adapter_kernel(
    win_ref, wout_ref, in_ref, cot_ref, out_ref,
    raw, flat, units, maps, edge, cols, prod, beside, down, uflat, utap, upk, grad, ghalo, gsend, grecv, gcol, shifted, lhs,
    rsend, rrecv, usend, urecv, zrecv, psend, precv, xsend, xrecv, hsend, hrecv, lsem,
):
    row, col = lax.axis_index("row"), lax.axis_index("col")
    h, x = row // 4, row % 4
    z, l, c = col // 4, (col // 2) % 2, col % 2
    y, zp = 2 * h + l, z % 2
    quarter, to_quarter = 2 * zp + l, z // 2
    both, no = jnp.logical_and, jnp.logical_not

    def at(xx, yy, zz, cc):
        return ((yy // 2) * 4 + xx, zz * 4 + (yy % 2) * 2 + cc)

    def along_x(d):
        return at((x + d) % 4, y, z, c)

    def along_y(d):
        return at(x, (y + d + 8) % 8, z, c)

    partner = at(x, y, z, 1 - c)
    carriers = [
        (kk, at(x, 2 * h + to_quarter % 2, to_quarter // 2 + 2 * k, kk),
         both(both(to_quarter // 2 + 2 * k == z, to_quarter % 2 == l), c == kk))
        for k in range(4) for kk in range(2)
    ]
    carried = [
        (i, cc, at(x, 2 * h + i % 2, 2 * quarter + i // 2, cc),
         both(both(2 * quarter + i // 2 == z, i % 2 == l), c == cc))
        for i in range(4) for cc in range(2)
    ]

    has_up, has_down, has_left, has_right = row > 0, row < 15, col > 0, col < 31
    around = [
        (has_up, (row - 1, col)), (has_down, (row + 1, col)),
        (has_left, (row, col - 1)), (has_right, (row, col + 1)),
        (both(has_up, has_left), (row - 1, col - 1)), (both(has_up, has_right), (row - 1, col + 1)),
        (both(has_down, has_left), (row + 1, col - 1)), (both(has_down, has_right), (row + 1, col + 1)),
    ]
    opposite = (1, 0, 3, 2, 7, 6, 5, 4)

    barrier = pltpu.get_barrier_semaphore()
    peers = [along_x(d) for d in (1, 2, 3)] + [along_y(d) for d in (1, -1, 2, -2)]
    peers += [at(x, y, (z + d) % 8, c) for d in (1, 7)] + [partner]
    for peer in peers:
        pl.semaphore_signal(barrier, inc=1, device_id=peer, device_id_type=MESH)
    for _, _, device, itself in carried:
        @pl.when(no(itself))
        def _():
            pl.semaphore_signal(barrier, inc=1, device_id=device, device_id_type=MESH)
    for exists, device in around:
        @pl.when(exists)
        def _():
            pl.semaphore_signal(barrier, inc=1, device_id=device, device_id_type=MESH)
    arrivals = sum(exists.astype(jnp.int32) for exists, _ in around)
    arrivals += sum(no(itself).astype(jnp.int32) for _, _, itself in carriers)
    pl.semaphore_wait(barrier, len(peers) + arrivals)

    place = 2 * zp + l
    chunks = []
    for n, (kk, device, itself) in enumerate(carriers):
        source = (win_ref, wout_ref)[kk]
        copy = pltpu.make_async_remote_copy(
            src_ref=source, dst_ref=raw.at[place, c], send_sem=rsend.at[n], recv_sem=rrecv.at[place, c],
            device_id=device, device_id_type=MESH,
        )
        pl.when(no(itself))(copy.start)
        chunks.append((copy, no(itself)))
        pl.when(itself)(pltpu.make_async_copy(source, raw.at[place, c], lsem.at[0]).start)
    local = [
        pltpu.make_async_copy(ref, maps.at[n, :, 1:17], lsem.at[1 + n]) for n, ref in enumerate((in_ref, cot_ref))
    ]
    for copy in local:
        copy.start()

    def map_row(n, d, ref):
        return pltpu.make_async_remote_copy(
            src_ref=ref.at[:, 15 * d], dst_ref=maps.at[n, :, 17 - 17 * d],
            send_sem=xsend.at[n, d], recv_sem=xrecv.at[n, opposite[d]],
            device_id=around[d][1], device_id_type=MESH,
        )

    def map_row_in(n, d, ref):
        return pltpu.make_async_remote_copy(
            src_ref=ref.at[:, 0], dst_ref=maps.at[n, :, 17 * d],
            send_sem=xsend.at[n, d], recv_sem=xrecv.at[n, d],
            device_id=around[d][1], device_id_type=MESH,
        )

    def border_rows():
        for n, ref in enumerate((in_ref, cot_ref)):
            for d in range(2):
                pl.when(around[d][0])(map_row(n, d, ref).start)

                @pl.when(jnp.logical_not(around[d][0]))
                def _():
                    maps[n, :, 17 * d] = jnp.zeros((4, 8, C), jnp.bfloat16)

    border_rows()
    for i, cc, _, itself in carried:
        pl.when(no(itself))(pltpu.make_async_remote_copy(
            src_ref=raw.at[i, cc], dst_ref=raw.at[i, cc], send_sem=rsend.at[0], recv_sem=rrecv.at[i, cc],
            device_id=partner, device_id_type=MESH,
        ).wait_recv)
        pl.when(itself)(pltpu.make_async_copy(win_ref, raw.at[i, cc], lsem.at[0]).wait)

    lanes = lax.broadcasted_iota(jnp.int32, (23, 128), 1)
    pieces = []
    for i in range(4):
        even = raw[i, 0].astype(jnp.float32)
        odd = pltpu.roll(raw[i, 1].astype(jnp.float32), 64, 1)
        low = jnp.concatenate([even[22:23], odd[0:22]], axis=0)
        pieces.append((even[0:22], jnp.where(lanes < 64, low, odd[0:23])))
    flat[...] = jnp.zeros((FRAME, 128), jnp.float32)
    for k in range(4):
        @pl.when(quarter == k)
        def _():
            for i in range(4):
                first = 4 * k + 45 * i
                flat[first:first + 22] = pieces[i][0]
                flat[first + 22:first + 45] = pieces[i][1]
    units[c, x, y, zp] = flat[...].astype(jnp.bfloat16)

    def column(n, side):
        return pltpu.make_async_remote_copy(
            src_ref=edge.at[n, side], dst_ref=cols.at[n, 1 - side],
            send_sem=xsend.at[n, 2 + side], recv_sem=xrecv.at[n, 3 - side],
            device_id=around[2 + side][1], device_id_type=MESH,
        )

    def column_in(n, side):
        return pltpu.make_async_remote_copy(
            src_ref=edge.at[n, side], dst_ref=cols.at[n, side],
            send_sem=xsend.at[n, 2 + side], recv_sem=xrecv.at[n, 2 + side],
            device_id=around[2 + side][1], device_id_type=MESH,
        )

    def border_columns():
        wanted = lax.broadcasted_iota(jnp.int32, (160, 576), 0)
        wanted = jnp.where(wanted < 80, wanted * 8, (wanted - 80) * 8 + 7)
        pick = jnp.where(lax.broadcasted_iota(jnp.int32, (160, 576), 1) == wanted, 1.0, 0.0).astype(jnp.bfloat16)
        for n, ref in enumerate((in_ref, cot_ref)):
            local[n].wait()
            for d in range(2):
                pl.when(around[d][0])(map_row_in(n, d, ref).wait_recv)
            picked = jnp.dot(pick, maps[n].reshape(576, C), preferred_element_type=jnp.float32)
            edge[n] = picked.astype(jnp.bfloat16).reshape(2, 80, C)

    def border_sends():
        for n in range(2):
            for side in range(2):
                pl.when(around[2 + side][0])(column(n, side).start)

                @pl.when(jnp.logical_not(around[2 + side][0]))
                def _():
                    cols[n, side] = jnp.zeros((80, C), jnp.bfloat16)

    waits = []

    def send(unit, device, sends, receives, when):
        copy = pltpu.make_async_remote_copy(
            src_ref=unit, dst_ref=unit, send_sem=sends, recv_sem=receives,
            device_id=device, device_id_type=MESH,
        )
        if when is None:
            copy.start()
        else:
            pl.when(when)(copy.start)
        waits.append((copy, when))

    def arrived(unit, receives):
        pltpu.make_async_remote_copy(
            src_ref=unit, dst_ref=unit, send_sem=psend.at[0], recv_sem=receives,
            device_id=partner, device_id_type=MESH,
        ).wait_recv()

    def share(n, xx, yy, parity):
        send(units.at[c, xx, yy, parity], partner, psend.at[n], precv.at[xx, yy, parity], None)

    def from_z(n):
        dx, dy = ORDER[n]
        xx, yy = (x + dx) % 4, (y + dy + 8) % 8
        arrived(units.at[c, xx, yy, 1 - zp], zrecv.at[xx, yy])
        share(32 + n, xx, yy, 1 - zp)

    first, second = c == 0, c == 1
    for n, (dx, dy) in enumerate(ORDER):
        xx, yy = (x + dx) % 4, (y + dy + 8) % 8
        parity = (xx + yy) % 2
        unit = units.at[c, xx, yy, zp]
        if n:
            arrived(unit, urecv.at[xx, yy])
        steps = {0: (1, -1, 2, -2), -2: (1, 2), 2: (-1, -2)}.get(dy, ())
        for k, step in enumerate(steps):
            when = None if dx == 0 else first
            if dy and abs(step) == 2:
                chosen = parity == (0 if step > 0 else 1)
                when = chosen if when is None else both(when, chosen)
            send(unit, along_y(step), usend.at[n, k], urecv.at[xx, yy], when)
        if dx == 0:
            for k, step in enumerate((1, 3, 2)):
                send(unit, along_x(step), usend.at[n, 4 + k], urecv.at[xx, yy], None if dy == 0 else second)
        send(unit, at(x, y, (z + 1 + 6 * parity) % 8, c), usend.at[n, 7], zrecv.at[xx, yy], None)
        share(n, xx, yy, zp)
        if n == 0:
            border_columns()
        if n == 20:
            border_sends()
        if n >= LAG:
            from_z(n - LAG)
    for n in range(32 - LAG, 32):
        from_z(n)
    for xx in range(4):
        for yy in range(8):
            for parity in range(2):
                arrived(units.at[1 - c, xx, yy, parity], precv.at[xx, yy, parity])

    frame_row = lax.broadcasted_iota(jnp.int32, (16, 128), 0)
    for k, whole in enumerate((down, uflat)):
        for g in range(16):
            frames = [units.at[k, g % 4, 2 * (g // 4) + q % 2, q // 2] for q in range(4)]
            for q in range(4):
                start = 720 * g + 176 * q
                last = FRAME if q == 3 else 176
                begin = 16 if q else 0
                whole[start + begin:start + last] = frames[q][begin:last]
                if q:
                    seam = jnp.where(
                        frame_row < 4 * q, frames[q - 1][176:192].astype(jnp.float32),
                        frames[q][0:16].astype(jnp.float32),
                    )
                    whole[start:start + 16] = seam.astype(jnp.bfloat16)
    down[11520:12800] = jnp.zeros((1280, 128), jnp.bfloat16)

    def up_tap(tap, carry):
        utap[...] = uflat[pl.ds(pl.multiple_of(tap * 1280, 1280), 1280)].astype(jnp.float32)
        for j in range(10):
            rows = utap[pl.ds(j, 128, stride=10), :].astype(jnp.bfloat16)
            upk[pl.ds(pl.multiple_of((8 - tap) * 128, 128), 128), 128 * j:128 * j + 128] = rows
        return carry

    lax.fori_loop(0, 9, up_tap, 0)
    upk[1152:1280] = jnp.zeros((128, C), jnp.bfloat16)
    for n in range(2):
        for side in range(2):
            pl.when(around[2 + side][0])(column_in(n, side).wait_recv)

    pixels = [
        jnp.concatenate([maps[n].reshape(576, C), cols[n].reshape(160, C)], axis=0) for n in range(2)
    ]

    def two_taps(step, carry):
        first = pl.multiple_of(step * 2560, 2560)
        two = jnp.concatenate([down[pl.ds(first, C)], down[pl.ds(first + C, C)]], axis=1)
        out = pl.ds(pl.multiple_of(step * 256, 256), 256)
        prod[0, :, out] = jnp.dot(pixels[0], two, preferred_element_type=jnp.float32)
        rows = upk[pl.ds(pl.multiple_of(step * 256, 256), 256)]
        prod[1, :, out] = lax.dot_general(
            pixels[1], rows, (((1,), (1,)), ((), ())), preferred_element_type=jnp.float32
        )
        return carry

    lax.fori_loop(0, 5, two_taps, 0)

    lane_row = lax.broadcasted_iota(jnp.int32, (8, 128), 0)
    for n in range(2):
        for side in range(2):
            three = [
                prod[n, 576 + 80 * side:656 + 80 * side, 128 * (3 * a + 2 * side):128 * (3 * a + 2 * side) + 128]
                for a in range(3)
            ]
            for b in range(4):
                terms = [three[a][18 * b + a:18 * b + a + 16] for a in range(3)]
                beside[n, side, 16 * b:16 * b + 16] = terms[0] + terms[1] + terms[2]

    def pixel_row(i):
        b, r = i // 16, i % 16
        sums = []
        for n in range(2):
            three = []
            for e in range(3):
                terms = [
                    prod[n, pl.ds(pl.multiple_of((b * 18 + r + a) * 8, 8), 8), 128 * (3 * a + e):128 * (3 * a + e) + 128]
                    for a in range(3)
                ]
                three.append(terms[0] + terms[1] + terms[2])
            sides = [beside[n, side, pl.ds(i, 1)] for side in range(2)]
            sums.append(
                jnp.where(lane_row == 0, sides[0], pltpu.roll(three[0], 1, 0))
                + three[1]
                + jnp.where(lane_row == 7, sides[1], pltpu.roll(three[2], 7, 0))
            )
        pre, back = sums
        s = jax.nn.sigmoid(pre)
        value = (back * (s * (1.0 + pre * (1.0 - s)))).astype(jnp.bfloat16)
        grad[b, 1 + r] = value
        value = value.astype(jnp.float32)
        gcol[0, pl.ds(i, 1)] = value[0:1]
        gcol[1, pl.ds(i, 1)] = value[7:8]

    for k in range(8):
        pixel_row((k // 2) * 16 + (k % 2) * 15)

    for side in range(2):
        for k in range(2):
            corner = [gcol[side, 16 * b + 15 * k:16 * b + 15 * k + 1] for b in range(4)]
            corner = jnp.concatenate(corner + [jnp.zeros((12, 128), jnp.float32)], axis=0)
            gsend[2 + 2 * k + side, 0:16] = corner.astype(jnp.bfloat16)

    def grad_border(d, to):
        if d < 2:
            src, dst = grad.at[:, 1 + 15 * d], grad.at[:, 17 - 17 * d]
            if not to:
                dst = grad.at[:, 17 * d]
        elif d < 4:
            src = gsend.at[d - 2, 0:64]
            dst = grecv.at[(3 - d) if to else (d - 2), 0:64]
        else:
            src = gsend.at[d - 2, 0:16]
            dst = grecv.at[(opposite[d] if to else d) - 2, 0:16]
        return pltpu.make_async_remote_copy(
            src_ref=src, dst_ref=dst, send_sem=hsend.at[d], recv_sem=hrecv.at[opposite[d] if to else d],
            device_id=around[d][1], device_id_type=MESH,
        )

    for d in (4, 5, 6, 7, 0, 1):
        pl.when(around[d][0])(grad_border(d, True).start)

    def seven_rows(k, carry):
        for u in range(7):
            pixel_row((k // 2) * 16 + (k % 2) * 7 + 1 + u)
        return carry

    lax.fori_loop(0, 8, seven_rows, 0)
    for side in range(2):
        gsend[side] = gcol[side, 0:64].astype(jnp.bfloat16)
        pl.when(around[2 + side][0])(grad_border(2 + side, True).start)
    for d in range(8):
        @pl.when(jnp.logical_not(around[d][0]))
        def _():
            if d < 2:
                grad[:, 17 * d] = jnp.zeros((4, 8, 128), jnp.bfloat16)
            elif d < 4:
                grecv[d - 2] = jnp.zeros((64, 128), jnp.bfloat16)
            else:
                grecv[d - 2, 0:16] = jnp.zeros((16, 128), jnp.bfloat16)
    for d in range(8):
        pl.when(around[d][0])(grad_border(d, False).wait_recv)

    for side in range(2):
        middle = grecv[side].astype(jnp.float32)
        top = grecv[2 + side, 0:16].astype(jnp.float32)
        bottom = grecv[4 + side, 0:16].astype(jnp.float32)
        for b in range(4):
            ghalo[side, 18 * b:18 * b + 18] = jnp.concatenate(
                [top[b:b + 1], middle[16 * b:16 * b + 16], bottom[b:b + 1]], axis=0
            )

    def shift_row(i):
        b, r = i // 18, i % 18
        value = grad[b, r].astype(jnp.float32)
        before, after = ghalo[0, pl.ds(i, 1)], ghalo[1, pl.ds(i, 1)]
        shifted[0, b, r] = jnp.where(lane_row == 7, after, pltpu.roll(value, 7, 0)).astype(jnp.bfloat16)
        shifted[1, b, r] = grad[b, r]
        shifted[2, b, r] = jnp.where(lane_row == 0, before, pltpu.roll(value, 1, 0)).astype(jnp.bfloat16)

    def nine_rows(k, carry):
        for u in range(9):
            shift_row(k * 9 + u)
        return carry

    lax.fori_loop(0, 8, nine_rows, 0)
    for tap in range(9):
        a, e = divmod(tap, 3)
        lhs[:, 128 * tap:128 * tap + 128] = shifted[e, :, 2 - a:18 - a].reshape(512, 128)

    def channels(step, carry):
        first = pl.multiple_of(step * 256, 256)
        weights = jnp.concatenate(
            [down[pl.ds(pl.multiple_of(C * tap + first, 256), 256)] for tap in range(9)], axis=1
        )
        out = lax.dot_general(lhs[...], weights, (((1,), (1,)), ((), ())), preferred_element_type=jnp.float32)
        kept = maps[1, :, 1:17, :, pl.ds(first, 256)].reshape(512, 256).astype(jnp.float32)
        out_ref[:, pl.ds(first, 256)] = (out + kept).astype(jnp.bfloat16)
        return carry

    lax.fori_loop(0, 5, channels, 0)
    for copy, when in chunks + waits:
        if when is None:
            copy.wait_send()
        else:
            pl.when(when)(copy.wait_send)
    for n, ref in enumerate((in_ref, cot_ref)):
        for d in range(2):
            pl.when(around[d][0])(map_row(n, d, ref).wait_send)
            pl.when(around[2 + d][0])(column(n, d).wait_send)
    for d in range(8):
        pl.when(around[d][0])(grad_border(d, True).wait_send)


def solution(mesh):
    dma = pltpu.SemaphoreType.DMA
    bf16, f32 = jnp.bfloat16, jnp.float32

    def shards(inputs, cotangent, w_in, w_out):
        chunks = [jnp.pad(w, (0, CHUNK * 128 - 2880)).reshape(CHUNK, 128) for w in (w_in, w_out)]
        result = pl.pallas_call(
            adapter_kernel,
            out_shape=jax.ShapeDtypeStruct((512, C), bf16),
            in_specs=[
                pl.BlockSpec(memory_space=pltpu.VMEM),
                pl.BlockSpec(memory_space=pltpu.VMEM),
                pl.BlockSpec(memory_space=pltpu.HBM),
                pl.BlockSpec(memory_space=pltpu.HBM),
            ],
            out_specs=pl.BlockSpec(memory_space=pltpu.VMEM),
            scratch_shapes=[
                pltpu.VMEM((4, 2, CHUNK, 128), bf16),
                pltpu.VMEM((FRAME, 128), f32),
                pltpu.VMEM((2, 4, 8, 2, FRAME, 128), bf16),
                pltpu.VMEM((2, 4, 18, 8, C), bf16),
                pltpu.VMEM((2, 2, 80, C), bf16),
                pltpu.VMEM((2, 2, 80, C), bf16),
                pltpu.VMEM((2, 736, 1280), f32),
                pltpu.VMEM((2, 2, 64, 128), f32),
                pltpu.VMEM((12800, 128), bf16),
                pltpu.VMEM((11520, 128), bf16),
                pltpu.VMEM((1280, 128), f32),
                pltpu.VMEM((1280, C), bf16),
                pltpu.VMEM((4, 18, 8, 128), bf16),
                pltpu.VMEM((2, 72, 128), f32),
                pltpu.VMEM((6, 64, 128), bf16),
                pltpu.VMEM((6, 64, 128), bf16),
                pltpu.VMEM((2, 64, 128), f32),
                pltpu.VMEM((3, 4, 18, 8, 128), bf16),
                pltpu.VMEM((512, 1152), bf16),
                dma((8,)), dma((4, 2)), dma((32, 8)), dma((4, 8)), dma((4, 8)), dma((64,)), dma((4, 8, 2)),
                dma((2, 4)), dma((2, 4)), dma((8,)), dma((8,)), dma((3,)),
            ],
            compiler_params=pltpu.CompilerParams(
                collective_id=0, has_side_effects=True, vmem_limit_bytes=44 << 20
            ),
        )(*chunks, *(pltpu.with_memory_space_constraint(m, pltpu.HBM) for m in (inputs, cotangent)))
        return result.reshape(4, 16, 8, C)

    spec = P(None, "row", "col", None)
    flat = P(("row", "col"))
    return jax.shard_map(
        shards, mesh=mesh, in_specs=(spec, spec, flat, flat), out_specs=spec, check_vma=False
    )
```

```python
import jax
import jax.numpy as jnp
from jax import lax
from jax.experimental import pallas as pl
from jax.experimental.pallas import tpu as pltpu
from jax.sharding import PartitionSpec as P

C = 1280
MESH = pl.DeviceIdType.MESH
CHUNK = 24
FRAME = 192
LAG = 12

ORDER = [
    (0, 0),
    (1, 0), (3, 0), (0, 1), (0, -1), (2, 0), (0, 2), (0, -2),
    (1, 1), (1, -1), (3, 1), (3, -1), (1, 2), (1, -2), (3, 2), (3, -2),
    (2, 1), (2, -1), (2, 2), (2, -2), (0, 3), (0, -3), (0, 4),
    (1, 3), (1, -3), (3, 3), (3, -3), (2, 3), (2, -3), (1, 4), (3, 4), (2, 4),
]


def adapter_kernel(
    win_ref, wout_ref, in_ref, cot_ref, out_ref,
    raw, flat, units, maps, edge, cols, prod, outside, beside, down, uflat, utap, upk, grad, ghalo, gsend, grecv, gcol, shifted, lhs,
    rsend, rrecv, usend, urecv, zrecv, psend, precv, xsend, xrecv, hsend, hrecv, lsem,
):
    row, col = lax.axis_index("row"), lax.axis_index("col")
    h, x = row // 4, row % 4
    z, l, c = col // 4, (col // 2) % 2, col % 2
    y, zp = 2 * h + l, z % 2
    quarter, to_quarter = 2 * zp + l, z // 2
    both, no = jnp.logical_and, jnp.logical_not

    def at(xx, yy, zz, cc):
        return ((yy // 2) * 4 + xx, zz * 4 + (yy % 2) * 2 + cc)

    def along_x(d):
        return at((x + d) % 4, y, z, c)

    def along_y(d):
        return at(x, (y + d + 8) % 8, z, c)

    partner = at(x, y, z, 1 - c)
    carriers = [
        (kk, at(x, 2 * h + to_quarter % 2, to_quarter // 2 + 2 * k, kk),
         both(both(to_quarter // 2 + 2 * k == z, to_quarter % 2 == l), c == kk))
        for k in range(4) for kk in range(2)
    ]
    carried = [
        (i, cc, at(x, 2 * h + i % 2, 2 * quarter + i // 2, cc),
         both(both(2 * quarter + i // 2 == z, i % 2 == l), c == cc))
        for i in range(4) for cc in range(2)
    ]

    has_up, has_down, has_left, has_right = row > 0, row < 15, col > 0, col < 31
    around = [
        (has_up, (row - 1, col)), (has_down, (row + 1, col)),
        (has_left, (row, col - 1)), (has_right, (row, col + 1)),
        (both(has_up, has_left), (row - 1, col - 1)), (both(has_up, has_right), (row - 1, col + 1)),
        (both(has_down, has_left), (row + 1, col - 1)), (both(has_down, has_right), (row + 1, col + 1)),
    ]
    opposite = (1, 0, 3, 2, 7, 6, 5, 4)

    barrier = pltpu.get_barrier_semaphore()
    peers = [along_x(d) for d in (1, 2, 3)] + [along_y(d) for d in (1, -1, 2, -2)]
    peers += [at(x, y, (z + d) % 8, c) for d in (1, 7)] + [partner]
    for peer in peers:
        pl.semaphore_signal(barrier, inc=1, device_id=peer, device_id_type=MESH)
    for _, _, device, itself in carried:
        @pl.when(no(itself))
        def _():
            pl.semaphore_signal(barrier, inc=1, device_id=device, device_id_type=MESH)
    for exists, device in around:
        @pl.when(exists)
        def _():
            pl.semaphore_signal(barrier, inc=1, device_id=device, device_id_type=MESH)
    arrivals = sum(exists.astype(jnp.int32) for exists, _ in around)
    arrivals += sum(no(itself).astype(jnp.int32) for _, _, itself in carriers)
    pl.semaphore_wait(barrier, len(peers) + arrivals)

    place = 2 * zp + l
    chunks = []
    for n, (kk, device, itself) in enumerate(carriers):
        source = (win_ref, wout_ref)[kk]
        copy = pltpu.make_async_remote_copy(
            src_ref=source, dst_ref=raw.at[place, c], send_sem=rsend.at[n], recv_sem=rrecv.at[place, c],
            device_id=device, device_id_type=MESH,
        )
        pl.when(no(itself))(copy.start)
        chunks.append((copy, no(itself)))
        pl.when(itself)(pltpu.make_async_copy(source, raw.at[place, c], lsem.at[0]).start)
    local = [
        pltpu.make_async_copy(ref, maps.at[n, :, 1:17], lsem.at[1 + n]) for n, ref in enumerate((in_ref, cot_ref))
    ]
    for copy in local:
        copy.start()

    def map_row(n, d, ref):
        return pltpu.make_async_remote_copy(
            src_ref=ref.at[:, 15 * d], dst_ref=maps.at[n, :, 17 - 17 * d],
            send_sem=xsend.at[n, d], recv_sem=xrecv.at[n, opposite[d]],
            device_id=around[d][1], device_id_type=MESH,
        )

    def map_row_in(n, d, ref):
        return pltpu.make_async_remote_copy(
            src_ref=ref.at[:, 0], dst_ref=maps.at[n, :, 17 * d],
            send_sem=xsend.at[n, d], recv_sem=xrecv.at[n, d],
            device_id=around[d][1], device_id_type=MESH,
        )

    def border_rows():
        for n, ref in enumerate((in_ref, cot_ref)):
            for d in range(2):
                pl.when(around[d][0])(map_row(n, d, ref).start)

                @pl.when(jnp.logical_not(around[d][0]))
                def _():
                    maps[n, :, 17 * d] = jnp.zeros((4, 8, C), jnp.bfloat16)

    border_rows()
    for i, cc, _, itself in carried:
        pl.when(no(itself))(pltpu.make_async_remote_copy(
            src_ref=raw.at[i, cc], dst_ref=raw.at[i, cc], send_sem=rsend.at[0], recv_sem=rrecv.at[i, cc],
            device_id=partner, device_id_type=MESH,
        ).wait_recv)
        pl.when(itself)(pltpu.make_async_copy(win_ref, raw.at[i, cc], lsem.at[0]).wait)

    lanes = lax.broadcasted_iota(jnp.int32, (23, 128), 1)
    pieces = []
    for i in range(4):
        even = raw[i, 0].astype(jnp.float32)
        odd = pltpu.roll(raw[i, 1].astype(jnp.float32), 64, 1)
        low = jnp.concatenate([even[22:23], odd[0:22]], axis=0)
        pieces.append((even[0:22], jnp.where(lanes < 64, low, odd[0:23])))
    flat[...] = jnp.zeros((FRAME, 128), jnp.float32)
    for k in range(4):
        @pl.when(quarter == k)
        def _():
            for i in range(4):
                first = 4 * k + 45 * i
                flat[first:first + 22] = pieces[i][0]
                flat[first + 22:first + 45] = pieces[i][1]
    units[c, x, y, zp] = flat[...].astype(jnp.bfloat16)

    def column(n, side):
        return pltpu.make_async_remote_copy(
            src_ref=edge.at[n, side], dst_ref=cols.at[n, 1 - side],
            send_sem=xsend.at[n, 2 + side], recv_sem=xrecv.at[n, 3 - side],
            device_id=around[2 + side][1], device_id_type=MESH,
        )

    def column_in(n, side):
        return pltpu.make_async_remote_copy(
            src_ref=edge.at[n, side], dst_ref=cols.at[n, side],
            send_sem=xsend.at[n, 2 + side], recv_sem=xrecv.at[n, 2 + side],
            device_id=around[2 + side][1], device_id_type=MESH,
        )

    def border_columns():
        wanted = lax.broadcasted_iota(jnp.int32, (160, 576), 0)
        wanted = jnp.where(wanted < 80, wanted * 8, (wanted - 80) * 8 + 7)
        pick = jnp.where(lax.broadcasted_iota(jnp.int32, (160, 576), 1) == wanted, 1.0, 0.0).astype(jnp.bfloat16)
        for n, ref in enumerate((in_ref, cot_ref)):
            local[n].wait()
            for d in range(2):
                pl.when(around[d][0])(map_row_in(n, d, ref).wait_recv)
            picked = jnp.dot(pick, maps[n].reshape(576, C), preferred_element_type=jnp.float32)
            edge[n] = picked.astype(jnp.bfloat16).reshape(2, 80, C)

    def border_sends():
        for n in range(2):
            for side in range(2):
                pl.when(around[2 + side][0])(column(n, side).start)

                @pl.when(jnp.logical_not(around[2 + side][0]))
                def _():
                    cols[n, side] = jnp.zeros((80, C), jnp.bfloat16)

    waits = []

    def send(unit, device, sends, receives, when):
        copy = pltpu.make_async_remote_copy(
            src_ref=unit, dst_ref=unit, send_sem=sends, recv_sem=receives,
            device_id=device, device_id_type=MESH,
        )
        if when is None:
            copy.start()
        else:
            pl.when(when)(copy.start)
        waits.append((copy, when))

    def arrived(unit, receives):
        pltpu.make_async_remote_copy(
            src_ref=unit, dst_ref=unit, send_sem=psend.at[0], recv_sem=receives,
            device_id=partner, device_id_type=MESH,
        ).wait_recv()

    def share(n, xx, yy, parity):
        send(units.at[c, xx, yy, parity], partner, psend.at[n], precv.at[xx, yy, parity], None)

    def from_z(n):
        dx, dy = ORDER[n]
        xx, yy = (x + dx) % 4, (y + dy + 8) % 8
        arrived(units.at[c, xx, yy, 1 - zp], zrecv.at[xx, yy])
        share(32 + n, xx, yy, 1 - zp)

    first, second = c == 0, c == 1
    for n, (dx, dy) in enumerate(ORDER):
        xx, yy = (x + dx) % 4, (y + dy + 8) % 8
        parity = (xx + yy) % 2
        unit = units.at[c, xx, yy, zp]
        if n:
            arrived(unit, urecv.at[xx, yy])
        steps = {0: (1, -1, 2, -2), -2: (1, 2), 2: (-1, -2)}.get(dy, ())
        for k, step in enumerate(steps):
            when = None if dx == 0 else first
            if dy and abs(step) == 2:
                chosen = parity == (0 if step > 0 else 1)
                when = chosen if when is None else both(when, chosen)
            send(unit, along_y(step), usend.at[n, k], urecv.at[xx, yy], when)
        if dx == 0:
            for k, step in enumerate((1, 3, 2)):
                send(unit, along_x(step), usend.at[n, 4 + k], urecv.at[xx, yy], None if dy == 0 else second)
        send(unit, at(x, y, (z + 1 + 6 * parity) % 8, c), usend.at[n, 7], zrecv.at[xx, yy], None)
        share(n, xx, yy, zp)
        if n == 0:
            border_columns()
        if n == 20:
            border_sends()
        if n >= LAG:
            from_z(n - LAG)
    for n in range(32 - LAG, 32):
        from_z(n)
    for xx in range(4):
        for yy in range(8):
            for parity in range(2):
                arrived(units.at[1 - c, xx, yy, parity], precv.at[xx, yy, parity])

    frame_row = lax.broadcasted_iota(jnp.int32, (16, 128), 0)
    for k, whole in enumerate((down, uflat)):
        for g in range(16):
            frames = [units.at[k, g % 4, 2 * (g // 4) + q % 2, q // 2] for q in range(4)]
            for q in range(4):
                start = 720 * g + 176 * q
                last = FRAME if q == 3 else 176
                begin = 16 if q else 0
                whole[start + begin:start + last] = frames[q][begin:last]
                if q:
                    seam = jnp.where(
                        frame_row < 4 * q, frames[q - 1][176:192].astype(jnp.float32),
                        frames[q][0:16].astype(jnp.float32),
                    )
                    whole[start:start + 16] = seam.astype(jnp.bfloat16)

    def up_tap(tap, carry):
        utap[...] = uflat[pl.ds(pl.multiple_of(tap * 1280, 1280), 1280)].astype(jnp.float32)
        for j in range(10):
            rows = utap[pl.ds(j, 128, stride=10), :].astype(jnp.bfloat16)
            upk[pl.ds(pl.multiple_of((8 - tap) * 128, 128), 128), 128 * j:128 * j + 128] = rows
        return carry

    lax.fori_loop(0, 9, up_tap, 0)
    for n in range(2):
        for side in range(2):
            pl.when(around[2 + side][0])(column_in(n, side).wait_recv)

    reach = [(0, 16, (0,)), (0, 17, (0, 1)), (1, 17, (1,)), (2, 18, (0,)), (2, 18, (1,))]
    for step, (low, high, sides) in enumerate(reach):
        taps = [tap for tap in (2 * step, 2 * step + 1) if tap < 9]
        out = slice(256 * step, 256 * step + 128 * len(taps))
        count = 32 * (high - low)
        for n in range(2):
            pixels = jnp.concatenate(
                [maps[n, :, low:high].reshape(count, C)] + [cols[n, side] for side in sides], axis=0
            )
            if n == 0:
                two = jnp.concatenate([down[C * tap:C * tap + C] for tap in taps], axis=1)
                value = jnp.dot(pixels, two, preferred_element_type=jnp.float32)
            else:
                value = lax.dot_general(
                    pixels, upk[out], (((1,), (1,)), ((), ())), preferred_element_type=jnp.float32
                )
            prod[n, :, low:high, :, out] = value[:count].reshape(4, high - low, 8, 128 * len(taps))
            for k, side in enumerate(sides):
                outside[n, side, :, out] = value[count + 80 * k:count + 80 * k + 80]

    lane_row = lax.broadcasted_iota(jnp.int32, (8, 128), 0)
    for n in range(2):
        for side in range(2):
            three = [
                outside[n, side, :, 128 * (3 * a + 2 * side):128 * (3 * a + 2 * side) + 128]
                for a in range(3)
            ]
            for b in range(4):
                terms = [three[a][18 * b + a:18 * b + a + 16] for a in range(3)]
                beside[n, side, 16 * b:16 * b + 16] = terms[0] + terms[1] + terms[2]

    def pixel_row(i):
        b, r = i // 16, i % 16
        sums = []
        for n in range(2):
            three = []
            for e in range(3):
                terms = [
                    prod[n, b, r + a, :, 128 * (3 * a + e):128 * (3 * a + e) + 128]
                    for a in range(3)
                ]
                three.append(terms[0] + terms[1] + terms[2])
            sides = [beside[n, side, pl.ds(i, 1)] for side in range(2)]
            sums.append(
                jnp.where(lane_row == 0, sides[0], pltpu.roll(three[0], 1, 0))
                + three[1]
                + jnp.where(lane_row == 7, sides[1], pltpu.roll(three[2], 7, 0))
            )
        pre, back = sums
        s = jax.nn.sigmoid(pre)
        value = (back * (s * (1.0 + pre * (1.0 - s)))).astype(jnp.bfloat16)
        grad[b, 1 + r] = value
        value = value.astype(jnp.float32)
        gcol[0, pl.ds(i, 1)] = value[0:1]
        gcol[1, pl.ds(i, 1)] = value[7:8]

    for k in range(8):
        pixel_row((k // 2) * 16 + (k % 2) * 15)

    for side in range(2):
        for k in range(2):
            corner = [gcol[side, 16 * b + 15 * k:16 * b + 15 * k + 1] for b in range(4)]
            corner = jnp.concatenate(corner + [jnp.zeros((12, 128), jnp.float32)], axis=0)
            gsend[2 + 2 * k + side, 0:16] = corner.astype(jnp.bfloat16)

    def grad_border(d, to):
        if d < 2:
            src, dst = grad.at[:, 1 + 15 * d], grad.at[:, 17 - 17 * d]
            if not to:
                dst = grad.at[:, 17 * d]
        elif d < 4:
            src = gsend.at[d - 2, 0:64]
            dst = grecv.at[(3 - d) if to else (d - 2), 0:64]
        else:
            src = gsend.at[d - 2, 0:16]
            dst = grecv.at[(opposite[d] if to else d) - 2, 0:16]
        return pltpu.make_async_remote_copy(
            src_ref=src, dst_ref=dst, send_sem=hsend.at[d], recv_sem=hrecv.at[opposite[d] if to else d],
            device_id=around[d][1], device_id_type=MESH,
        )

    for d in (4, 5, 6, 7, 0, 1):
        pl.when(around[d][0])(grad_border(d, True).start)

    def seven_rows(k, carry):
        for u in range(7):
            pixel_row((k // 2) * 16 + (k % 2) * 7 + 1 + u)
        return carry

    lax.fori_loop(0, 8, seven_rows, 0)
    for side in range(2):
        gsend[side] = gcol[side, 0:64].astype(jnp.bfloat16)
        pl.when(around[2 + side][0])(grad_border(2 + side, True).start)
    for d in range(8):
        @pl.when(jnp.logical_not(around[d][0]))
        def _():
            if d < 2:
                grad[:, 17 * d] = jnp.zeros((4, 8, 128), jnp.bfloat16)
            elif d < 4:
                grecv[d - 2] = jnp.zeros((64, 128), jnp.bfloat16)
            else:
                grecv[d - 2, 0:16] = jnp.zeros((16, 128), jnp.bfloat16)
    for d in range(8):
        pl.when(around[d][0])(grad_border(d, False).wait_recv)

    for side in range(2):
        middle = grecv[side].astype(jnp.float32)
        top = grecv[2 + side, 0:16].astype(jnp.float32)
        bottom = grecv[4 + side, 0:16].astype(jnp.float32)
        for b in range(4):
            ghalo[side, 18 * b:18 * b + 18] = jnp.concatenate(
                [top[b:b + 1], middle[16 * b:16 * b + 16], bottom[b:b + 1]], axis=0
            )

    def shift_row(i):
        b, r = i // 18, i % 18
        value = grad[b, r].astype(jnp.float32)
        before, after = ghalo[0, pl.ds(i, 1)], ghalo[1, pl.ds(i, 1)]
        shifted[0, b, r] = jnp.where(lane_row == 7, after, pltpu.roll(value, 7, 0)).astype(jnp.bfloat16)
        shifted[1, b, r] = grad[b, r]
        shifted[2, b, r] = jnp.where(lane_row == 0, before, pltpu.roll(value, 1, 0)).astype(jnp.bfloat16)

    def nine_rows(k, carry):
        for u in range(9):
            shift_row(k * 9 + u)
        return carry

    lax.fori_loop(0, 8, nine_rows, 0)
    for tap in range(9):
        a, e = divmod(tap, 3)
        lhs[:, 128 * tap:128 * tap + 128] = shifted[e, :, 2 - a:18 - a].reshape(512, 128)

    def channels(step, carry):
        first = pl.multiple_of(step * 256, 256)
        weights = jnp.concatenate(
            [down[pl.ds(pl.multiple_of(C * tap + first, 256), 256)] for tap in range(9)], axis=1
        )
        out = lax.dot_general(lhs[...], weights, (((1,), (1,)), ((), ())), preferred_element_type=jnp.float32)
        kept = maps[1, :, 1:17, :, pl.ds(first, 256)].reshape(512, 256).astype(jnp.float32)
        out_ref[:, pl.ds(first, 256)] = (out + kept).astype(jnp.bfloat16)
        return carry

    lax.fori_loop(0, 5, channels, 0)
    for copy, when in chunks + waits:
        if when is None:
            copy.wait_send()
        else:
            pl.when(when)(copy.wait_send)
    for n, ref in enumerate((in_ref, cot_ref)):
        for d in range(2):
            pl.when(around[d][0])(map_row(n, d, ref).wait_send)
            pl.when(around[2 + d][0])(column(n, d).wait_send)
    for d in range(8):
        pl.when(around[d][0])(grad_border(d, True).wait_send)


def solution(mesh):
    dma = pltpu.SemaphoreType.DMA
    bf16, f32 = jnp.bfloat16, jnp.float32

    def shards(inputs, cotangent, w_in, w_out):
        chunks = [jnp.pad(w, (0, CHUNK * 128 - 2880)).reshape(CHUNK, 128) for w in (w_in, w_out)]
        result = pl.pallas_call(
            adapter_kernel,
            out_shape=jax.ShapeDtypeStruct((512, C), bf16),
            in_specs=[
                pl.BlockSpec(memory_space=pltpu.VMEM),
                pl.BlockSpec(memory_space=pltpu.VMEM),
                pl.BlockSpec(memory_space=pltpu.HBM),
                pl.BlockSpec(memory_space=pltpu.HBM),
            ],
            out_specs=pl.BlockSpec(memory_space=pltpu.VMEM),
            scratch_shapes=[
                pltpu.VMEM((4, 2, CHUNK, 128), bf16),
                pltpu.VMEM((FRAME, 128), f32),
                pltpu.VMEM((2, 4, 8, 2, FRAME, 128), bf16),
                pltpu.VMEM((2, 4, 18, 8, C), bf16),
                pltpu.VMEM((2, 2, 80, C), bf16),
                pltpu.VMEM((2, 2, 80, C), bf16),
                pltpu.VMEM((2, 4, 18, 8, 1152), f32),
                pltpu.VMEM((2, 2, 80, 1152), f32),
                pltpu.VMEM((2, 2, 64, 128), f32),
                pltpu.VMEM((11520, 128), bf16),
                pltpu.VMEM((11520, 128), bf16),
                pltpu.VMEM((1280, 128), f32),
                pltpu.VMEM((1152, C), bf16),
                pltpu.VMEM((4, 18, 8, 128), bf16),
                pltpu.VMEM((2, 72, 128), f32),
                pltpu.VMEM((6, 64, 128), bf16),
                pltpu.VMEM((6, 64, 128), bf16),
                pltpu.VMEM((2, 64, 128), f32),
                pltpu.VMEM((3, 4, 18, 8, 128), bf16),
                pltpu.VMEM((512, 1152), bf16),
                dma((8,)), dma((4, 2)), dma((32, 8)), dma((4, 8)), dma((4, 8)), dma((64,)), dma((4, 8, 2)),
                dma((2, 4)), dma((2, 4)), dma((8,)), dma((8,)), dma((3,)),
            ],
            compiler_params=pltpu.CompilerParams(
                collective_id=0, has_side_effects=True, vmem_limit_bytes=44 << 20
            ),
        )(*chunks, *(pltpu.with_memory_space_constraint(m, pltpu.HBM) for m in (inputs, cotangent)))
        return result.reshape(4, 16, 8, C)

    spec = P(None, "row", "col", None)
    flat = P(("row", "col"))
    return jax.shard_map(
        shards, mesh=mesh, in_specs=(spec, spec, flat, flat), out_specs=spec, check_vma=False
    )
```

```python
import jax
import jax.numpy as jnp
from jax import lax
from jax.experimental import pallas as pl
from jax.experimental.pallas import tpu as pltpu
from jax.sharding import PartitionSpec as P

C = 1280
MESH = pl.DeviceIdType.MESH
CHUNK = 24
FRAME = 192
LAG = 12

ORDER = [
    (0, 0),
    (1, 0), (3, 0), (0, 1), (0, -1), (2, 0), (0, 2), (0, -2),
    (1, 1), (1, -1), (3, 1), (3, -1), (1, 2), (1, -2), (3, 2), (3, -2),
    (2, 1), (2, -1), (2, 2), (2, -2), (0, 3), (0, -3), (0, 4),
    (1, 3), (1, -3), (3, 3), (3, -3), (2, 3), (2, -3), (1, 4), (3, 4), (2, 4),
]


def adapter_kernel(
    win_ref, wout_ref, in_ref, cot_ref, out_ref,
    raw, flat, units, maps, edge, cols, prod, outside, beside, down, uflat, utap, upk, grad, ghalo, gsend, grecv, gcol, shifted, lhs,
    rsend, rrecv, usend, urecv, zrecv, psend, precv, xsend, xrecv, hsend, hrecv, lsem,
):
    row, col = lax.axis_index("row"), lax.axis_index("col")
    h, x = row // 4, row % 4
    z, l, c = col // 4, (col // 2) % 2, col % 2
    y, zp = 2 * h + l, z % 2
    quarter, to_quarter = 2 * zp + l, z // 2
    both, no = jnp.logical_and, jnp.logical_not

    def at(xx, yy, zz, cc):
        return ((yy // 2) * 4 + xx, zz * 4 + (yy % 2) * 2 + cc)

    def along_x(d):
        return at((x + d) % 4, y, z, c)

    def along_y(d):
        return at(x, (y + d + 8) % 8, z, c)

    partner = at(x, y, z, 1 - c)
    carriers = [
        (kk, at(x, 2 * h + to_quarter % 2, to_quarter // 2 + 2 * k, kk),
         both(both(to_quarter // 2 + 2 * k == z, to_quarter % 2 == l), c == kk))
        for k in range(4) for kk in range(2)
    ]
    carried = [
        (i, cc, at(x, 2 * h + i % 2, 2 * quarter + i // 2, cc),
         both(both(2 * quarter + i // 2 == z, i % 2 == l), c == cc))
        for i in range(4) for cc in range(2)
    ]

    has_up, has_down, has_left, has_right = row > 0, row < 15, col > 0, col < 31
    around = [
        (has_up, (row - 1, col)), (has_down, (row + 1, col)),
        (has_left, (row, col - 1)), (has_right, (row, col + 1)),
        (both(has_up, has_left), (row - 1, col - 1)), (both(has_up, has_right), (row - 1, col + 1)),
        (both(has_down, has_left), (row + 1, col - 1)), (both(has_down, has_right), (row + 1, col + 1)),
    ]
    opposite = (1, 0, 3, 2, 7, 6, 5, 4)

    barrier = pltpu.get_barrier_semaphore()
    peers = [along_x(d) for d in (1, 2, 3)] + [along_y(d) for d in (1, -1, 2, -2)]
    peers += [at(x, y, (z + d) % 8, c) for d in (1, 7)] + [partner]
    for peer in peers:
        pl.semaphore_signal(barrier, inc=1, device_id=peer, device_id_type=MESH)
    for _, _, device, itself in carried:
        @pl.when(no(itself))
        def _():
            pl.semaphore_signal(barrier, inc=1, device_id=device, device_id_type=MESH)
    for exists, device in around:
        @pl.when(exists)
        def _():
            pl.semaphore_signal(barrier, inc=1, device_id=device, device_id_type=MESH)
    arrivals = sum(exists.astype(jnp.int32) for exists, _ in around)
    arrivals += sum(no(itself).astype(jnp.int32) for _, _, itself in carriers)
    pl.semaphore_wait(barrier, len(peers) + arrivals)

    place = 2 * zp + l
    chunks = []
    for n, (kk, device, itself) in enumerate(carriers):
        source = (win_ref, wout_ref)[kk]
        copy = pltpu.make_async_remote_copy(
            src_ref=source, dst_ref=raw.at[place, c], send_sem=rsend.at[n], recv_sem=rrecv.at[place, c],
            device_id=device, device_id_type=MESH,
        )
        pl.when(no(itself))(copy.start)
        chunks.append((copy, no(itself)))
        pl.when(itself)(pltpu.make_async_copy(source, raw.at[place, c], lsem.at[0]).start)
    local = [
        pltpu.make_async_copy(ref, maps.at[n, :, 1:17], lsem.at[1 + n]) for n, ref in enumerate((in_ref, cot_ref))
    ]
    for copy in local:
        copy.start()

    def map_row(n, d, ref):
        return pltpu.make_async_remote_copy(
            src_ref=ref.at[:, 15 * d], dst_ref=maps.at[n, :, 17 - 17 * d],
            send_sem=xsend.at[n, d], recv_sem=xrecv.at[n, opposite[d]],
            device_id=around[d][1], device_id_type=MESH,
        )

    def map_row_in(n, d, ref):
        return pltpu.make_async_remote_copy(
            src_ref=ref.at[:, 0], dst_ref=maps.at[n, :, 17 * d],
            send_sem=xsend.at[n, d], recv_sem=xrecv.at[n, d],
            device_id=around[d][1], device_id_type=MESH,
        )

    def border_rows():
        for n, ref in enumerate((in_ref, cot_ref)):
            for d in range(2):
                pl.when(around[d][0])(map_row(n, d, ref).start)

                @pl.when(jnp.logical_not(around[d][0]))
                def _():
                    maps[n, :, 17 * d] = jnp.zeros((4, 8, C), jnp.bfloat16)

    border_rows()
    for i, cc, _, itself in carried:
        pl.when(no(itself))(pltpu.make_async_remote_copy(
            src_ref=raw.at[i, cc], dst_ref=raw.at[i, cc], send_sem=rsend.at[0], recv_sem=rrecv.at[i, cc],
            device_id=partner, device_id_type=MESH,
        ).wait_recv)
        pl.when(itself)(pltpu.make_async_copy(win_ref, raw.at[i, cc], lsem.at[0]).wait)

    lanes = lax.broadcasted_iota(jnp.int32, (23, 128), 1)
    pieces = []
    for i in range(4):
        even = raw[i, 0].astype(jnp.float32)
        odd = pltpu.roll(raw[i, 1].astype(jnp.float32), 64, 1)
        low = jnp.concatenate([even[22:23], odd[0:22]], axis=0)
        pieces.append((even[0:22], jnp.where(lanes < 64, low, odd[0:23])))
    flat[...] = jnp.zeros((FRAME, 128), jnp.float32)
    for k in range(4):
        @pl.when(quarter == k)
        def _():
            for i in range(4):
                first = 4 * k + 45 * i
                flat[first:first + 22] = pieces[i][0]
                flat[first + 22:first + 45] = pieces[i][1]
    units[c, x, y, zp] = flat[...].astype(jnp.bfloat16)

    def column(n, side):
        return pltpu.make_async_remote_copy(
            src_ref=edge.at[n, side], dst_ref=cols.at[n, 1 - side],
            send_sem=xsend.at[n, 2 + side], recv_sem=xrecv.at[n, 3 - side],
            device_id=around[2 + side][1], device_id_type=MESH,
        )

    def column_in(n, side):
        return pltpu.make_async_remote_copy(
            src_ref=edge.at[n, side], dst_ref=cols.at[n, side],
            send_sem=xsend.at[n, 2 + side], recv_sem=xrecv.at[n, 2 + side],
            device_id=around[2 + side][1], device_id_type=MESH,
        )

    def border_columns():
        wanted = lax.broadcasted_iota(jnp.int32, (160, 576), 0)
        wanted = jnp.where(wanted < 80, wanted * 8, (wanted - 80) * 8 + 7)
        pick = jnp.where(lax.broadcasted_iota(jnp.int32, (160, 576), 1) == wanted, 1.0, 0.0).astype(jnp.bfloat16)
        for n, ref in enumerate((in_ref, cot_ref)):
            local[n].wait()
            for d in range(2):
                pl.when(around[d][0])(map_row_in(n, d, ref).wait_recv)
            picked = jnp.dot(pick, maps[n].reshape(576, C), preferred_element_type=jnp.float32)
            edge[n] = picked.astype(jnp.bfloat16).reshape(2, 80, C)

    def border_sends():
        for n in range(2):
            for side in range(2):
                pl.when(around[2 + side][0])(column(n, side).start)

                @pl.when(jnp.logical_not(around[2 + side][0]))
                def _():
                    cols[n, side] = jnp.zeros((80, C), jnp.bfloat16)

    waits = []

    def send(unit, device, sends, receives, when):
        copy = pltpu.make_async_remote_copy(
            src_ref=unit, dst_ref=unit, send_sem=sends, recv_sem=receives,
            device_id=device, device_id_type=MESH,
        )
        if when is None:
            copy.start()
        else:
            pl.when(when)(copy.start)
        waits.append((copy, when))

    def arrived(unit, receives):
        pltpu.make_async_remote_copy(
            src_ref=unit, dst_ref=unit, send_sem=psend.at[0], recv_sem=receives,
            device_id=partner, device_id_type=MESH,
        ).wait_recv()

    def share(n, xx, yy, parity):
        send(units.at[c, xx, yy, parity], partner, psend.at[n], precv.at[xx, yy, parity], None)

    def from_z(n):
        dx, dy = ORDER[n]
        xx, yy = (x + dx) % 4, (y + dy + 8) % 8
        arrived(units.at[c, xx, yy, 1 - zp], zrecv.at[xx, yy])
        share(32 + n, xx, yy, 1 - zp)

    first, second = c == 0, c == 1
    for n, (dx, dy) in enumerate(ORDER):
        xx, yy = (x + dx) % 4, (y + dy + 8) % 8
        parity = (xx + yy) % 2
        unit = units.at[c, xx, yy, zp]
        if n:
            arrived(unit, urecv.at[xx, yy])
        steps = {0: (1, -1, 2, -2), -2: (1, 2), 2: (-1, -2)}.get(dy, ())
        for k, step in enumerate(steps):
            when = None if dx == 0 else first
            if dy and abs(step) == 2:
                chosen = parity == (0 if step > 0 else 1)
                when = chosen if when is None else both(when, chosen)
            send(unit, along_y(step), usend.at[n, k], urecv.at[xx, yy], when)
        if dx == 0:
            for k, step in enumerate((1, 3, 2)):
                send(unit, along_x(step), usend.at[n, 4 + k], urecv.at[xx, yy], None if dy == 0 else second)
        send(unit, at(x, y, (z + 1 + 6 * parity) % 8, c), usend.at[n, 7], zrecv.at[xx, yy], None)
        share(n, xx, yy, zp)
        if n == 0:
            border_columns()
        if n == 20:
            border_sends()
        if n >= LAG:
            from_z(n - LAG)
    for n in range(32 - LAG, 32):
        from_z(n)
    for xx in range(4):
        for yy in range(8):
            for parity in range(2):
                arrived(units.at[1 - c, xx, yy, parity], precv.at[xx, yy, parity])

    frame_row = lax.broadcasted_iota(jnp.int32, (16, 128), 0)
    for k, whole in enumerate((down, uflat)):
        for g in range(16):
            frames = [units.at[k, g % 4, 2 * (g // 4) + q % 2, q // 2] for q in range(4)]
            for q in range(4):
                start = 720 * g + 176 * q
                last = FRAME if q == 3 else 176
                begin = 16 if q else 0
                whole[start + begin:start + last] = frames[q][begin:last]
                if q:
                    seam = jnp.where(
                        frame_row < 4 * q, frames[q - 1][176:192].astype(jnp.float32),
                        frames[q][0:16].astype(jnp.float32),
                    )
                    whole[start:start + 16] = seam.astype(jnp.bfloat16)

    def up_tap(tap, carry):
        utap[...] = uflat[pl.ds(pl.multiple_of(tap * 1280, 1280), 1280)].astype(jnp.float32)
        for j in range(10):
            rows = utap[pl.ds(j, 128, stride=10), :].astype(jnp.bfloat16)
            upk[pl.ds(pl.multiple_of((8 - tap) * 128, 128), 128), 128 * j:128 * j + 128] = rows
        return carry

    lax.fori_loop(0, 9, up_tap, 0)
    for n in range(2):
        for side in range(2):
            pl.when(around[2 + side][0])(column_in(n, side).wait_recv)

    reach = [(0, 16, (0,)), (0, 17, (0, 1)), (1, 17, (1,)), (2, 18, (0,)), (2, 18, (1,))]
    for step, (low, high, sides) in enumerate(reach):
        taps = [tap for tap in (2 * step, 2 * step + 1) if tap < 9]
        out = slice(256 * step, 256 * step + 128 * len(taps))
        count = 32 * (high - low)
        for n in range(2):
            pixels = jnp.concatenate(
                [maps[n, :, low:high].reshape(count, C)] + [cols[n, side] for side in sides], axis=0
            )
            if n == 0:
                two = jnp.concatenate([down[C * tap:C * tap + C] for tap in taps], axis=1)
                value = jnp.dot(pixels, two, preferred_element_type=jnp.float32)
            else:
                value = lax.dot_general(
                    pixels, upk[out], (((1,), (1,)), ((), ())), preferred_element_type=jnp.float32
                )
            prod[n, :, low:high, :, out] = value[:count].reshape(4, high - low, 8, 128 * len(taps))
            for k, side in enumerate(sides):
                outside[n, side, :, out] = value[count + 80 * k:count + 80 * k + 80]

    lane_row = lax.broadcasted_iota(jnp.int32, (8, 128), 0)
    for n in range(2):
        for side in range(2):
            three = [
                outside[n, side, :, 128 * (3 * a + 2 * side):128 * (3 * a + 2 * side) + 128]
                for a in range(3)
            ]
            for b in range(4):
                terms = [three[a][18 * b + a:18 * b + a + 16] for a in range(3)]
                beside[n, side, 16 * b:16 * b + 16] = terms[0] + terms[1] + terms[2]

    def pixel_row(i):
        b, r = i // 16, i % 16
        sums = []
        for n in range(2):
            three = []
            for e in range(3):
                terms = [
                    prod[n, b, r + a, :, 128 * (3 * a + e):128 * (3 * a + e) + 128]
                    for a in range(3)
                ]
                three.append(terms[0] + terms[1] + terms[2])
            sides = [beside[n, side, pl.ds(i, 1)] for side in range(2)]
            sums.append(
                jnp.where(lane_row == 0, sides[0], pltpu.roll(three[0], 1, 0))
                + three[1]
                + jnp.where(lane_row == 7, sides[1], pltpu.roll(three[2], 7, 0))
            )
        pre, back = sums
        s = jax.nn.sigmoid(pre)
        value = (back * (s * (1.0 + pre * (1.0 - s)))).astype(jnp.bfloat16)
        grad[b, 1 + r] = value
        value = value.astype(jnp.float32)
        gcol[0, pl.ds(i, 1)] = value[0:1]
        gcol[1, pl.ds(i, 1)] = value[7:8]

    for k in range(8):
        pixel_row((k // 2) * 16 + (k % 2) * 15)

    for side in range(2):
        for k in range(2):
            corner = [gcol[side, 16 * b + 15 * k:16 * b + 15 * k + 1] for b in range(4)]
            corner = jnp.concatenate(corner + [jnp.zeros((12, 128), jnp.float32)], axis=0)
            gsend[2 + 2 * k + side, 0:16] = corner.astype(jnp.bfloat16)

    def grad_border(d, to):
        if d < 2:
            src, dst = grad.at[:, 1 + 15 * d], grad.at[:, 17 - 17 * d]
            if not to:
                dst = grad.at[:, 17 * d]
        elif d < 4:
            src = gsend.at[d - 2, 0:64]
            dst = grecv.at[(3 - d) if to else (d - 2), 0:64]
        else:
            src = gsend.at[d - 2, 0:16]
            dst = grecv.at[(opposite[d] if to else d) - 2, 0:16]
        return pltpu.make_async_remote_copy(
            src_ref=src, dst_ref=dst, send_sem=hsend.at[d], recv_sem=hrecv.at[opposite[d] if to else d],
            device_id=around[d][1], device_id_type=MESH,
        )

    for d in (4, 5, 6, 7, 0, 1):
        pl.when(around[d][0])(grad_border(d, True).start)

    def seven_rows(k, carry):
        for u in range(7):
            pixel_row((k // 2) * 16 + (k % 2) * 7 + 1 + u)
        return carry

    lax.fori_loop(0, 8, seven_rows, 0)
    for side in range(2):
        gsend[side] = gcol[side, 0:64].astype(jnp.bfloat16)
        pl.when(around[2 + side][0])(grad_border(2 + side, True).start)
    for d in range(8):
        @pl.when(jnp.logical_not(around[d][0]))
        def _():
            if d < 2:
                grad[:, 17 * d] = jnp.zeros((4, 8, 128), jnp.bfloat16)
            elif d < 4:
                grecv[d - 2] = jnp.zeros((64, 128), jnp.bfloat16)
            else:
                grecv[d - 2, 0:16] = jnp.zeros((16, 128), jnp.bfloat16)
    for d in range(8):
        pl.when(around[d][0])(grad_border(d, False).wait_recv)

    for side in range(2):
        middle = grecv[side].astype(jnp.float32)
        top = grecv[2 + side, 0:16].astype(jnp.float32)
        bottom = grecv[4 + side, 0:16].astype(jnp.float32)
        for b in range(4):
            ghalo[side, 18 * b:18 * b + 18] = jnp.concatenate(
                [top[b:b + 1], middle[16 * b:16 * b + 16], bottom[b:b + 1]], axis=0
            )

    def shift_row(i):
        b, r = i // 18, i % 18
        value = grad[b, r].astype(jnp.float32)
        before, after = ghalo[0, pl.ds(i, 1)], ghalo[1, pl.ds(i, 1)]
        shifted[0, b, r] = jnp.where(lane_row == 7, after, pltpu.roll(value, 7, 0)).astype(jnp.bfloat16)
        shifted[1, b, r] = grad[b, r]
        shifted[2, b, r] = jnp.where(lane_row == 0, before, pltpu.roll(value, 1, 0)).astype(jnp.bfloat16)

    def nine_rows(k, carry):
        for u in range(9):
            shift_row(k * 9 + u)
        return carry

    lax.fori_loop(0, 8, nine_rows, 0)
    for tap in range(9):
        a, e = divmod(tap, 3)
        lhs[:, 128 * tap:128 * tap + 128] = shifted[e, :, 2 - a:18 - a].reshape(512, 128)

    for first in range(0, C, 256):
        weights = jnp.concatenate([down[C * tap + first:C * tap + first + 256] for tap in range(9)], axis=1)
        out = lax.dot_general(lhs[...], weights, (((1,), (1,)), ((), ())), preferred_element_type=jnp.float32)
        kept = maps[1, :, 1:17, :, first:first + 256].reshape(512, 256).astype(jnp.float32)
        out_ref[:, first:first + 256] = (out + kept).astype(jnp.bfloat16)
    for copy, when in chunks + waits:
        if when is None:
            copy.wait_send()
        else:
            pl.when(when)(copy.wait_send)
    for n, ref in enumerate((in_ref, cot_ref)):
        for d in range(2):
            pl.when(around[d][0])(map_row(n, d, ref).wait_send)
            pl.when(around[2 + d][0])(column(n, d).wait_send)
    for d in range(8):
        pl.when(around[d][0])(grad_border(d, True).wait_send)


def solution(mesh):
    dma = pltpu.SemaphoreType.DMA
    bf16, f32 = jnp.bfloat16, jnp.float32

    def shards(inputs, cotangent, w_in, w_out):
        chunks = [jnp.pad(w, (0, CHUNK * 128 - 2880)).reshape(CHUNK, 128) for w in (w_in, w_out)]
        result = pl.pallas_call(
            adapter_kernel,
            out_shape=jax.ShapeDtypeStruct((512, C), bf16),
            in_specs=[
                pl.BlockSpec(memory_space=pltpu.VMEM),
                pl.BlockSpec(memory_space=pltpu.VMEM),
                pl.BlockSpec(memory_space=pltpu.HBM),
                pl.BlockSpec(memory_space=pltpu.HBM),
            ],
            out_specs=pl.BlockSpec(memory_space=pltpu.VMEM),
            scratch_shapes=[
                pltpu.VMEM((4, 2, CHUNK, 128), bf16),
                pltpu.VMEM((FRAME, 128), f32),
                pltpu.VMEM((2, 4, 8, 2, FRAME, 128), bf16),
                pltpu.VMEM((2, 4, 18, 8, C), bf16),
                pltpu.VMEM((2, 2, 80, C), bf16),
                pltpu.VMEM((2, 2, 80, C), bf16),
                pltpu.VMEM((2, 4, 18, 8, 1152), f32),
                pltpu.VMEM((2, 2, 80, 1152), f32),
                pltpu.VMEM((2, 2, 64, 128), f32),
                pltpu.VMEM((11520, 128), bf16),
                pltpu.VMEM((11520, 128), bf16),
                pltpu.VMEM((1280, 128), f32),
                pltpu.VMEM((1152, C), bf16),
                pltpu.VMEM((4, 18, 8, 128), bf16),
                pltpu.VMEM((2, 72, 128), f32),
                pltpu.VMEM((6, 64, 128), bf16),
                pltpu.VMEM((6, 64, 128), bf16),
                pltpu.VMEM((2, 64, 128), f32),
                pltpu.VMEM((3, 4, 18, 8, 128), bf16),
                pltpu.VMEM((512, 1152), bf16),
                dma((8,)), dma((4, 2)), dma((32, 8)), dma((4, 8)), dma((4, 8)), dma((64,)), dma((4, 8, 2)),
                dma((2, 4)), dma((2, 4)), dma((8,)), dma((8,)), dma((3,)),
            ],
            compiler_params=pltpu.CompilerParams(
                collective_id=0, has_side_effects=True, vmem_limit_bytes=44 << 20
            ),
        )(*chunks, *(pltpu.with_memory_space_constraint(m, pltpu.HBM) for m in (inputs, cotangent)))
        return result.reshape(4, 16, 8, C)

    spec = P(None, "row", "col", None)
    flat = P(("row", "col"))
    return jax.shard_map(
        shards, mesh=mesh, in_specs=(spec, spec, flat, flat), out_specs=spec, check_vma=False
    )
```
